256 devices in a mesh: tile: 64 (over z, x, core), chan: 4 (over y).
Axes of the slice: x: 4, y: 4, z: 8, core: 2. Of those that a mesh axis runs over, the one named last changes fastest.
Arguments:
- state: bfloat16 [40, 2048, 512], P(None, 'tile', 'chan'), may hold values from -6 to 6
- obs_values: bfloat16 [131072, 128], P(('tile', 'chan')), may hold values from -6 to 6
- obs_tile: int32 [131072, 1], P(('tile', 'chan')), may hold values from 0 to 63; in each aligned block of 512 rows (0 to 511, 512 to 1023, ...) at most 16 rows name the same one
- obs_cell: int32 [131072], P(('tile', 'chan')), may hold values from 0 to 1279
- neighbours: int32 [40, 8], replicated, may hold values from 0 to 15, as said below
- quadrature: float32 [3, 40, 8], replicated, may hold values from 0.1 to 0.6
- embed_weight: bfloat16 [128, 512], P(None, 'chan'), may hold values from -0.5 to 0.5
- disco_weight: bfloat16 [3, 128, 512], P(None, None, 'chan'), may hold values from -0.3125 to 0.3125
- cotangent: bfloat16 [40, 2048, 512], P(None, 'tile', 'chan'), may hold values from -6 to 6
Outputs:
- output: bfloat16 [40, 2048, 512], P(None, 'tile', 'chan')
- grad_state: bfloat16 [40, 2048, 512], P(None, 'tile', 'chan')
- grad_disco: float32 [3, 128, 512], P(None, None, 'chan')
- grad_obs: float32 [128, 512], P(None, 'chan')
The draws below stay inside these ranges and needn't reach their ends.
Inputs may be any that keep to these rules, and one draw needn't show every extreme that they name: `obs_tile`: the 512 rows of one device name any sector at most 16 times. `neighbours`: the value 15 marks an unused slot; the used slots of a row come first.
All inputs are finite; a program needn't handle non-finite values.
Results may differ from the reference program's by a relative error of at most 0.023.
Values may be sent and summed in bfloat16 or wider, within the bound.
No kernel may reach another device: no remote copies, remote signals or barrier semaphores. Data moves between devices by JAX's collectives and lax.ppermute only.
A program may use at most 64 MiB of HBM per device.

```python
import math
import jax
import jax.numpy as jnp
import numpy as np
from jax import lax

C = 512
GSIZE = 128
F = 128
K = 3
J = 8
RL = 2
NOFF = 15
LAT = 40
LON_T = 32
OBS_DEV = 512
NLON = 2048
NOBS = 131072
CAP = 16
N_TILE = 64


def draw_neighbours(key, part):
    offset_key = jax.random.fold_in(key, 11)
    length_key = jax.random.fold_in(key, 12)
    chosen = jax.random.randint(offset_key, (LAT, J), 0, NOFF)
    filled = jax.random.randint(length_key, (LAT, 1), 4, J + 1)
    filled = filled.at[0, 0].set(4)
    slot_index = jnp.arange(J, dtype=jnp.int32)[None, :]
    table = jnp.where(slot_index < filled, chosen, NOFF)
    table = table.at[0, 0].set(0)
    return table.astype(jnp.int32)


def set_ends(result, key, smallest, largest):
    dims = result.shape
    place = [jax.random.randint(jax.random.fold_in(key, axis), (), 0, dims[axis]) for axis in range(len(dims))]
    result = result.at[tuple(place)].set(smallest)
    longest = dims.index(max(dims))
    place[longest] = (place[longest] + 1) % dims[longest]
    return result.at[tuple(place)].set(largest)


def block_levels(rng, extent, split, low, high):
    factor_of, own = 1.0, jax.random.fold_in(rng, 6)
    for position, shards_of in split:
        draws = jnp.exp(jax.random.uniform(jax.random.fold_in(own, position), (shards_of,), jnp.float32, low / len(split), high / len(split)))
        factor_of = factor_of * jnp.repeat(draws, extent[position] // shards_of).reshape([-1 if axis == position else 1 for axis in range(len(extent))])
    return factor_of


def deal_out(stream_key, own, number, rows, count, top, most, lean):
    order = jax.random.permutation(stream_key, count)
    heavy_load, usual = load_shares(count, rows * top, most, lean, True), load_shares(count, rows * top, most, lean, False)
    places = jnp.arange(count)

    def named(lengths, turn):
        used = int((lengths > 0).sum())
        fixed = max(1, used // 4)
        moved = fixed + (places - fixed + turn * (used - fixed)) % max(1, count - fixed)
        return jnp.zeros((count,), jnp.int32).at[order[jnp.where(places < fixed, places, moved)]].set(jnp.asarray(lengths, jnp.int32))

    lengths = jnp.where(number % 4 == 0, named(heavy_load, number // 4), named(usual, number - number // 4 - 1))
    mixed = jax.random.permutation(jax.random.fold_in(own, 3), count)
    donor, receiver = mixed[0:count // 2 * 2:2], mixed[1:count // 2 * 2:2]
    slack = jnp.minimum(lengths[donor] - 1, most - lengths[receiver]) // 2
    slack = jnp.where((donor == order[0]) | (receiver == order[0]) | (lengths[receiver] == 0), 0, jnp.maximum(slack, 0))
    moved = jax.random.randint(jax.random.fold_in(own, 4), (count // 2,), 0, 1 << 20) % (slack + 1)
    lengths = lengths.at[donor].add(-moved).at[receiver].add(moved)
    items = jnp.searchsorted(jnp.cumsum(lengths), jnp.arange(rows * top), side="right").astype(jnp.int32)
    grid = items.reshape(top, rows).T
    grid = grid[jax.random.permutation(jax.random.fold_in(own, 1), rows)]
    turn = jax.random.randint(jax.random.fold_in(own, 2), (rows, 1), 0, top)
    return jnp.take_along_axis(grid, (jnp.arange(top)[None, :] + turn) % top, axis=1)


def load_shares(amount, total, bound, skew, full):
    weights = [(1 << 20) // math.isqrt(rank ** skew) + 1 for rank in range(1, amount + 1)]
    largest = bound if full else min(bound, max(-(-total // amount), total * weights[0] // sum(weights)))
    least = 1 if total - largest >= amount - 1 else 0
    counts, rest = [largest] + [least] * (amount - 1), total - largest - least * (amount - 1)
    while rest > 0:
        movable = [i for i in range(1, amount) if counts[i] < largest] or [i for i in range(1, amount) if counts[i] < bound]
        mass, left = sum([weights[i] for i in movable]), rest
        for i in movable:
            more = min(bound - counts[i], max(1, left * weights[i] // mass), rest)
            counts[i] = counts[i] + more
            rest = rest - more
    return np.array(counts)


def noise(own_key, shape, scale, reach, cuts=(), kind=jnp.bfloat16):
    result = scale * jax.random.normal(own_key, shape, jnp.float32)
    if cuts:
        result = result * block_levels(own_key, shape, cuts, -0.22, 0.18)
    return jnp.clip(result, -reach, reach).astype(kind)


def setup_inputs(seed: int = 0) -> dict:
    key_list = jax.random.split(jax.random.key(seed), 10)
    state = noise(key_list[0], (LAT, NLON, C), 1.0, 6.0, ((1, 64), (2, 4)))
    obs_values = noise(key_list[1], (NOBS, F), 1.0, 6.0, ((0, 256),))
    obs_tile_keys = jax.random.split(jax.random.fold_in(key_list[2], 1), NOBS // OBS_DEV)
    obs_tile_turns = jax.random.permutation(jax.random.fold_in(key_list[2], 3), NOBS // OBS_DEV)
    obs_tile = jax.vmap(lambda own, number: deal_out(jax.random.fold_in(key_list[2], 2), own, number, OBS_DEV, N_TILE, 1, CAP, 2))(obs_tile_keys, obs_tile_turns).reshape((NOBS, 1))
    obs_cell = set_ends(jax.random.randint(key_list[3], (NOBS,), 0, LAT * LON_T), jax.random.fold_in(key_list[3], 1), 0, (LAT * LON_T) - 1).astype(jnp.int32)
    neighbours = draw_neighbours(jax.random.fold_in(key_list[9], 71), 0)
    quadrature = jnp.clip(jnp.exp(jax.random.uniform(key_list[5], (K, LAT, J), jnp.float32, math.log(0.1), math.log(0.6))), 0.1, 0.6)
    embed_weight = noise(key_list[6], (F, C), F ** -0.5, 0.5, ((1, 4),))
    disco_weight = noise(key_list[7], (K, GSIZE, C), (K * GSIZE) ** -0.5, 0.3125, ((2, 4),))
    cotangent = noise(key_list[8], (LAT, NLON, C), 1.0, 6.0, ((1, 64), (2, 4)))
    return {"state": state, "obs_values": obs_values, "obs_tile": obs_tile, "obs_cell": obs_cell, "neighbours": neighbours, "quadrature": quadrature, "embed_weight": embed_weight, "disco_weight": disco_weight, "cotangent": cotangent}


tanh_scale = 0.7978845608028654
cubic_weight = 0.044715


def gelu_value(value_in):
    return 0.5 * value_in * (1.0 + jnp.tanh(tanh_scale * (value_in + cubic_weight * value_in * value_in * value_in)))


def gelu_slope(value_in):
    inner = jnp.tanh(tanh_scale * (value_in + cubic_weight * value_in * value_in * value_in))
    return 0.5 * (1.0 + inner) + 0.5 * value_in * (1.0 - inner * inner) * tanh_scale * (1.0 + 3.0 * cubic_weight * value_in * value_in)


def widen(grid_field):
    wrapped = jnp.concatenate([grid_field[:, -RL:], grid_field, grid_field[:, :RL]], axis=1)
    return jnp.pad(wrapped, ((1, 1), (0, 0), (0, 0)))


def reference(state, obs_values, obs_tile, obs_cell, neighbours, quadrature, embed_weight, disco_weight, cotangent):
    span_width = 2 * RL + 1
    groups = C // GSIZE
    target_cell = ((obs_cell // LON_T) * NLON + obs_tile[:, 0] * LON_T + obs_cell % LON_T).astype(jnp.int32)
    slot_picks = (neighbours[:, :, None] == jnp.arange(NOFF, dtype=jnp.int32)[None, None, :]).astype(jnp.float32)
    coupling = jnp.einsum("kij,ijo->kio", quadrature, slot_picks, precision=lax.Precision.HIGHEST)
    coupling_pad = jnp.pad(coupling, ((0, 0), (1, 1), (0, 0)))
    state_groups = jnp.moveaxis(state.reshape(LAT, NLON, groups, GSIZE), 2, 0)
    cot_groups = jnp.moveaxis(cotangent.reshape(LAT, NLON, groups, GSIZE), 2, 0)
    embed_groups = jnp.moveaxis(embed_weight.reshape(F, groups, GSIZE), 1, 0)
    disco_groups = jnp.moveaxis(disco_weight.reshape(K, GSIZE, groups, GSIZE), 2, 0)

    def one_group(group_parts):
        state_part, cot_part, embed_part, disco_part = group_parts
        embedded = jnp.dot(obs_values, embed_part, preferred_element_type=jnp.float32).astype(jnp.bfloat16)
        deposit = jnp.zeros((LAT * NLON, GSIZE), jnp.float32).at[target_cell].add(embedded.astype(jnp.float32))
        mixed_in = (state_part.astype(jnp.float32) + deposit.reshape(LAT, NLON, GSIZE)).astype(jnp.bfloat16)
        padded = widen(mixed_in).astype(jnp.float32)
        basis_list = []
        before = jnp.zeros((LAT, NLON, GSIZE), jnp.float32)
        for kernel_index in range(K):
            accumulated = jnp.zeros((LAT, NLON, GSIZE), jnp.float32)
            for offset in range(NOFF):
                row_shift = offset // span_width - 1
                col_shift = offset % span_width - RL
                window = padded[1 + row_shift:1 + row_shift + LAT, RL + col_shift:RL + col_shift + NLON]
                accumulated = accumulated + coupling[kernel_index, :, offset][:, None, None] * window
            basis_term = accumulated.astype(jnp.bfloat16)
            basis_list.append(basis_term)
            before = before + jnp.einsum("ila,ab->ilb", basis_term.astype(jnp.float32), disco_part[kernel_index].astype(jnp.float32))
        output = (mixed_in.astype(jnp.float32) + gelu_value(before)).astype(jnp.bfloat16)
        slope_back = (cot_part.astype(jnp.float32) * gelu_slope(before)).astype(jnp.bfloat16)
        slope_wide = slope_back.astype(jnp.float32)
        spread = cot_part.astype(jnp.float32)
        weight_rows = []
        for kernel_index in range(K):
            weight_rows.append(jnp.einsum("ila,ilb->ab", basis_list[kernel_index].astype(jnp.float32), slope_wide))
            back_basis = jnp.einsum("ilb,ab->ila", slope_wide, disco_part[kernel_index].astype(jnp.float32)).astype(jnp.bfloat16)
            back_pad = widen(back_basis).astype(jnp.float32)
            for offset in range(NOFF):
                row_shift = offset // span_width - 1
                col_shift = offset % span_width - RL
                source = back_pad[1 - row_shift:1 - row_shift + LAT, RL - col_shift:RL - col_shift + NLON]
                factor = coupling_pad[kernel_index, 1 - row_shift:1 - row_shift + LAT, offset]
                spread = spread + factor[:, None, None] * source
        grad_part = spread.astype(jnp.bfloat16)
        rows_grad = grad_part.reshape(LAT * NLON, GSIZE)[target_cell]
        embed_grad = jnp.dot(obs_values.T, rows_grad, preferred_element_type=jnp.float32)
        return output, grad_part, jnp.stack(weight_rows), embed_grad

    outputs, grads, weight_parts, embed_parts = lax.map(one_group, (state_groups, cot_groups, embed_groups, disco_groups))
    output = jnp.moveaxis(outputs, 0, 2).reshape(LAT, NLON, C)
    grad_state = jnp.moveaxis(grads, 0, 2).reshape(LAT, NLON, C)
    grad_disco = jnp.moveaxis(weight_parts, 0, 2).reshape(K, GSIZE, C) * (LAT * NLON) ** -0.5
    grad_obs = jnp.moveaxis(embed_parts, 0, 1).reshape(F, C) * NOBS ** -0.5
    return (output, grad_state, grad_disco, grad_obs)
```

```python
import functools

import jax
import jax.numpy as jnp
from jax import lax
from jax.experimental import pallas as pl
from jax.experimental.pallas import tpu as pltpu
from jax.sharding import PartitionSpec as P

K = 3
J = 8
LAT = 40
LON = 32
CH = 128
CELLS = LAT * LON
ROWS = 512
TILES = 64
CAP = 16
SLOT = 18
PACK = TILES * SLOT
BF = jnp.bfloat16
F32 = jnp.float32
tanh_scale = 0.7978845608028654
cubic_weight = 0.044715
GRID_SCALE = float(CELLS * TILES) ** -0.5
OBS_SCALE = float(ROWS * TILES * 4) ** -0.5

VM = pl.BlockSpec(memory_space=pltpu.VMEM)


def call(body, outs, n_in, scratch=(), flops=0, bytes_accessed=0, name=None):
    return pl.pallas_call(
        body,
        out_shape=outs,
        in_specs=[VM] * n_in,
        out_specs=jax.tree.map(lambda _: VM, outs),
        scratch_shapes=list(scratch),
        compiler_params=pltpu.CompilerParams(vmem_limit_bytes=32 << 20),
        cost_estimate=pl.CostEstimate(
            flops=flops, bytes_accessed=bytes_accessed, transcendentals=0
        ),
        name=name,
    )


def sds(shape, dtype):
    return jax.ShapeDtypeStruct(shape, dtype)


def iota(shape, dim):
    return lax.broadcasted_iota(jnp.int32, shape, dim)


def one(mask):
    return jnp.where(mask, 1.0, 0.0).astype(BF)


def dot(a, b, ca=1, cb=0):
    return lax.dot_general(a, b, (((ca,), (cb,)), ((), ())), preferred_element_type=F32)


def pack_body(obs_ref, tile_ref, cell_ref, out_ref):
    tile = tile_ref[...]
    cell = cell_ref[...]
    named = iota((TILES, ROWS), 0) == tile
    onehot = one(named)
    before = one(iota((ROWS, ROWS), 0) < iota((ROWS, ROWS), 1))
    counts = dot(onehot, before)
    rank = jnp.sum(jnp.where(named, counts, 0.0), axis=0, keepdims=True).astype(jnp.int32)
    place = one(iota((PACK, ROWS), 0) == tile * SLOT + rank)
    high = (cell >> 5).astype(F32)
    low = (cell & 31).astype(F32)
    lane = iota((CH, ROWS), 0)
    marks = jnp.where(lane == rank, high, 0.0) + jnp.where(lane == rank + CAP, low, 0.0)
    marks = dot(onehot, marks.astype(BF), 1, 1)
    mark_place = one(iota((PACK, TILES), 0) == iota((PACK, TILES), 1) * SLOT + CAP)
    packed = dot(place, obs_ref[...]) + dot(mark_place, marks.astype(BF))
    out_ref[...] = packed.astype(BF)


def add_block(block_ref, store):
    block = block_ref[...]
    q = iota((CH, PACK), 1)
    t18 = iota((CH, PACK), 0) * SLOT
    marks = dot(one(q == t18 + CAP), block)
    marks = marks.T.astype(BF)
    spread = one((q >= t18) & (q < t18 + SLOT))
    wide = dot(marks[: 2 * CAP], spread)
    qf = iota((CAP, PACK), 1).astype(F32)
    within = qf - SLOT * jnp.floor((qf + 0.5) * (1.0 / SLOT))
    mine = within == iota((CAP, PACK), 0).astype(F32)
    high = jnp.sum(jnp.where(mine, wide[:CAP], 0.0), axis=0, keepdims=True)
    low = jnp.sum(jnp.where(mine, wide[CAP:], 0.0), axis=0, keepdims=True)
    high = jnp.where(within[:1] > CAP - 0.5, -1.0, high)
    lows = jnp.where(iota((LON, PACK), 0).astype(F32) == low, 1.0, 0.0)
    for c in range(0, LAT, 8):
        hot = jnp.concatenate(
            [jnp.where(high == float(i), lows, 0.0).astype(BF) for i in range(c, c + 8)], axis=0
        )
        store(slice(c * LON, (c + 8) * LON), dot(hot, block))


def deposit_first(block_ref, acc_ref):
    def store(rows, part):
        acc_ref[rows] = part

    add_block(block_ref, store)


def deposit_next(block_ref, acc_in, acc_ref):
    def store(rows, part):
        acc_ref[rows] = acc_in[rows] + part

    add_block(block_ref, store)


def deposit_last(block_ref, acc_in, state_ref, we_ref, mixed_ref, a_ref, left_ref, right_ref):
    we = we_ref[...]

    def store(rows, part):
        total = acc_in[rows] + part
        a = total.astype(BF)
        a_ref[rows] = a
        mixed = state_ref[rows].astype(F32) + dot(a, we)
        mixed_ref[rows] = mixed.astype(BF)
        lat = slice(rows.start // LON, rows.stop // LON)
        m3 = mixed.reshape(8, LON, CH)
        a3 = total.reshape(8, LON, CH)
        left_ref[lat] = jnp.concatenate([m3[:, :2], a3[:, :2]], axis=1).astype(BF)
        right_ref[lat] = jnp.concatenate([m3[:, LON - 2 :], a3[:, LON - 2 :]], axis=1).astype(BF)

    add_block(block_ref, store)


def filter_body(quad_ref, near_ref, m_ref, mt_ref, v_ref):
    quad = quad_ref[...]
    near = near_ref[...]
    near = jnp.concatenate([near] * K, axis=0)
    lane = iota((K * LAT, CH), 1)
    coupling = jnp.zeros((K * LAT, CH), F32)
    for j in range(J):
        coupling += jnp.where(near[:, j : j + 1] == lane, quad[:, j : j + 1], 0.0)
    coupling = coupling.astype(BF)

    def column(at):
        edge = at - 96
        step = jnp.where(at < 96, at >> 5, edge >> 2)
        side = edge & 3
        col = jnp.where(at < 96, at & 31, jnp.where(side < 2, side - 2, side + 30))
        return step, jnp.where(at < 108, col, -99)

    step, _ = column(iota((CH, CH), 1))
    for b in range(5):
        v_ref[:, b * CH : (b + 1) * CH] = dot(coupling, one(iota((CH, CH), 0) == step * 5 + b))
    _, col = column(iota((LON, CH), 1))
    masks = [
        jnp.where(col == iota((LON, CH), 0) + (b - 2), 1.0, 0.0) for b in range(5)
    ]

    def one_row(i, _):
        parts = []
        for k in range(K):
            row = v_ref[pl.ds(k * LAT + i, 1), :]
            part = masks[0] * row[:, :CH]
            for b in range(1, 5):
                part += masks[b] * row[:, b * CH : (b + 1) * CH]
            parts.append(part)
        whole = jnp.concatenate(parts, axis=0)
        m_ref[i] = whole.astype(BF)
        whole = jnp.concatenate([whole, jnp.zeros((CH - K * LON, CH), F32)], axis=0)
        mt_ref[i] = whole.T.astype(BF)
        return 0

    lax.fori_loop(0, LAT, one_row, 0)


def block_body(
    m_ref, mt_ref, mixed_ref, a_ref, left_ref, right_ref, cot_ref, wd_ref,
    out_ref, gs_ref, el_ref, er_ref, g_ref,
    xp, hx, basis, bgs, tp, h3,
):
    xp[:LON] = jnp.zeros((LON, CH), BF)
    xp[LON : LON + CELLS] = mixed_ref[...]
    xp[LON + CELLS :] = jnp.zeros((LON, CH), BF)
    left = left_ref[...].astype(F32)
    right = right_ref[...].astype(F32)
    edge = jnp.concatenate([left[:, :2], right[:, :2]], axis=1)
    edge_a = jnp.concatenate([left[:, 2:], right[:, 2:], jnp.zeros((LAT, 4, CH), F32)], axis=1)
    none = jnp.zeros((1, 4, CH), F32)
    edge = jnp.concatenate([none, edge, none], axis=0)
    edge = jnp.concatenate(
        [edge[:LAT], edge[1 : LAT + 1], edge[2:], jnp.zeros((LAT, 20, CH), F32)], axis=1
    )
    hx[...] = edge.reshape(CELLS, CH).astype(BF)

    def gather(i, _):
        at = pl.multiple_of(i * LON, LON)
        near = jnp.concatenate([xp[pl.ds(at, 3 * LON)], hx[pl.ds(at, LON)]], axis=0)
        part = dot(m_ref[i], near).astype(BF)
        for k in range(K):
            basis[pl.ds(at, LON), k * CH : (k + 1) * CH] = part[k * LON : (k + 1) * LON]
        return 0

    lax.fori_loop(0, LAT, gather, 0, unroll=4)

    wd = wd_ref[...]
    gd = jnp.zeros((CH, K * CH), F32)
    for c in range(0, LAT, 8):
        rows = slice(c * LON, (c + 8) * LON)
        some = basis[rows]
        v = dot(some, wd)
        inner = jnp.tanh(tanh_scale * (v + cubic_weight * v * v * v))
        out_ref[rows] = (mixed_ref[rows].astype(F32) + 0.5 * v * (1.0 + inner)).astype(BF)
        rate = 0.5 * (1.0 + inner) + 0.5 * v * (1.0 - inner * inner) * tanh_scale * (
            1.0 + 3.0 * cubic_weight * v * v
        )
        slope = (cot_ref[rows].astype(F32) * rate).astype(BF)
        gd += dot(slope, some, 0, 0)
        back = dot(slope, wd, 1, 1).astype(BF)
        for i in range(8):
            at = (c + i) * CH
            for k in range(K):
                bgs[at + k * LON : at + (k + 1) * LON] = back[
                    i * LON : (i + 1) * LON, k * CH : (k + 1) * CH
                ]
            bgs[at + K * LON : at + CH] = jnp.zeros((CH - K * LON, CH), BF)

    tp[...] = jnp.zeros((CELLS + 2 * LON, CH), F32)

    def scatter(i, _):
        at = pl.multiple_of(i * LON, LON)
        part = dot(mt_ref[i], bgs[pl.ds(pl.multiple_of(i * CH, CH), CH)])
        tp[pl.ds(at, 3 * LON)] += part[: 3 * LON]
        h3[i] = part[3 * LON : 3 * LON + 16]
        return 0

    lax.fori_loop(0, LAT, scatter, 0, unroll=4)

    gs = cot_ref[...].astype(F32) + tp[LON : LON + CELLS]
    gs_ref[...] = gs
    pad = jnp.zeros((1, 16, CH), F32)
    side = jnp.concatenate([pad, h3[...], pad], axis=0)
    side = side[2:, 0:4] + side[1 : LAT + 1, 4:8] + side[:LAT, 8:12]
    el_ref[...] = side[:, :2]
    er_ref[...] = side[:, 2:]
    side = jnp.concatenate([side, jnp.zeros((LAT, 4, CH), F32)], axis=1)
    go = dot(a_ref[...], gs.astype(BF), 0, 0)
    go += dot(edge_a.reshape(8 * LAT, CH).astype(BF), side.reshape(8 * LAT, CH).astype(BF), 0, 0)
    g_ref[: K * CH] = (gd.T * GRID_SCALE).astype(BF)
    g_ref[K * CH :] = (go * OBS_SCALE).astype(BF)


def finish_body(gs_ref, from_left, from_right, out_ref):
    full = jnp.concatenate(
        [from_left[...], jnp.zeros((LAT, LON - 4, CH), F32), from_right[...]], axis=1
    )
    out_ref[...] = (gs_ref[...].reshape(LAT, LON, CH) + full).astype(BF)


def sum_body(parts_ref, out_ref):
    total = jnp.sum(parts_ref[...].astype(F32), axis=0, keepdims=True).astype(BF)
    out_ref[...] = jnp.broadcast_to(total.astype(F32), out_ref.shape).astype(BF)


def local(
    state, obs_values, obs_tile, obs_cell, neighbours, quadrature, embed_weight, disco_weight,
    cotangent,
):
    def shift(x, axis, by):
        count = lax.axis_size(axis)
        return lax.ppermute(x, axis, [(i, (i + by) % count) for i in range(count)])

    exchange = functools.partial(
        lax.all_to_all, axis_name="tile", split_axis=0, concat_axis=0, tiled=True
    )
    grid_rows = (CELLS, CH)
    packed = call(pack_body, sds((PACK, CH), BF), 3, flops=1 << 28, name="pack")(
        obs_values, obs_tile.reshape(1, ROWS), obs_cell.reshape(1, ROWS)
    )
    mine = exchange(packed.reshape(TILES, SLOT // 2, 2, CH)).reshape(PACK, CH)
    m, mt = call(
        filter_body,
        (sds((LAT, K * LON, CH), BF), sds((LAT, CH, CH), BF)),
        2,
        [pltpu.VMEM((K * LAT, 5 * CH), F32)],
        flops=1 << 26,
        bytes_accessed=1 << 22,
        name="filters",
    )(quadrature.reshape(K * LAT, J), neighbours)
    others = [shift(mine, "chan", by) for by in (1, 3, 2)]
    cost = dict(flops=2 * CELLS * PACK * CH, bytes_accessed=1 << 20)
    acc = call(deposit_first, sds(grid_rows, F32), 1, name="deposit", **cost)(mine)
    for block in others[:2]:
        acc = call(deposit_next, sds(grid_rows, F32), 2, name="deposit", **cost)(block, acc)
    mixed, a, left, right = call(
        deposit_last,
        (sds(grid_rows, BF), sds(grid_rows, BF), sds((LAT, 4, CH), BF), sds((LAT, 4, CH), BF)),
        4,
        name="mix",
        **cost,
    )(others[2], acc, state.reshape(grid_rows), embed_weight)
    from_left = shift(right, "tile", 1)
    from_right = shift(left, "tile", -1)
    output, gs, el, er, grads = call(
        block_body,
        (
            sds(grid_rows, BF),
            sds(grid_rows, F32),
            sds((LAT, 2, CH), F32),
            sds((LAT, 2, CH), F32),
            sds((K * CH + CH, CH), BF),
        ),
        8,
        [
            pltpu.VMEM((CELLS + 2 * LON, CH), BF),
            pltpu.VMEM(grid_rows, BF),
            pltpu.VMEM((CELLS, K * CH), BF),
            pltpu.VMEM((LAT * CH, CH), BF),
            pltpu.VMEM((CELLS + 2 * LON, CH), F32),
            pltpu.VMEM((LAT, 16, CH), F32),
        ],
        flops=1 << 30,
        bytes_accessed=1 << 22,
        name="block",
    )(
        m, mt, mixed, a, from_left, from_right, cotangent.reshape(grid_rows),
        disco_weight.reshape(K * CH, CH),
    )
    parts = exchange(grads.reshape(TILES, 8, CH))
    side_left = shift(er, "tile", 1)
    side_right = shift(el, "tile", -1)
    grad_state = call(finish_body, sds((LAT, LON, CH), BF), 3, bytes_accessed=1 << 20, name="finish")(
        gs, side_left, side_right
    )
    summed = call(sum_body, sds((TILES, 8, CH), BF), 1, bytes_accessed=1 << 18, name="sum")(parts)
    total = exchange(summed).reshape(K * CH + CH, CH).astype(F32)
    return (
        output.reshape(LAT, LON, CH),
        grad_state,
        total[: K * CH].reshape(K, CH, CH),
        total[K * CH :],
    )


def solution(mesh):
    in_specs = (
        P(None, "tile", "chan"),
        P(("tile", "chan"), None),
        P(("tile", "chan"), None),
        P(("tile", "chan")),
        P(),
        P(),
        P(None, "chan"),
        P(None, None, "chan"),
        P(None, "tile", "chan"),
    )
    out_specs = (
        P(None, "tile", "chan"),
        P(None, "tile", "chan"),
        P(None, None, "chan"),
        P(None, "chan"),
    )
    return jax.shard_map(local, mesh=mesh, in_specs=in_specs, out_specs=out_specs, check_vma=False)
```

```python
import functools

import jax
import jax.numpy as jnp
from jax import lax
from jax.experimental import pallas as pl
from jax.experimental.pallas import tpu as pltpu
from jax.sharding import PartitionSpec as P

K = 3
J = 8
LAT = 40
LON = 32
CH = 128
CELLS = LAT * LON
ROWS = 512
TILES = 64
CAP = 16
SLOT = 18
PACK = TILES * SLOT
BF = jnp.bfloat16
F32 = jnp.float32
tanh_scale = 0.7978845608028654
cubic_weight = 0.044715
GRID_SCALE = float(CELLS * TILES) ** -0.5
OBS_SCALE = float(ROWS * TILES * 4) ** -0.5

VM = pl.BlockSpec(memory_space=pltpu.VMEM)
SM = pl.BlockSpec(memory_space=pltpu.SMEM)


def call(body, outs, n_in, scratch=(), flops=0, bytes_accessed=0, name=None, space=VM, aliases=None, scalars=0, vmem=32):
    return pl.pallas_call(
        body,
        out_shape=outs,
        in_specs=[SM] * scalars + [space] * n_in,
        out_specs=jax.tree.map(lambda _: VM, outs),
        scratch_shapes=list(scratch),
        compiler_params=pltpu.CompilerParams(vmem_limit_bytes=vmem << 20),
        cost_estimate=pl.CostEstimate(
            flops=flops, bytes_accessed=bytes_accessed, transcendentals=0
        ),
        name=name,
        input_output_aliases=aliases or {},
    )


def sds(shape, dtype):
    return jax.ShapeDtypeStruct(shape, dtype)


def iota(shape, dim):
    return lax.broadcasted_iota(jnp.int32, shape, dim)


def one(mask):
    return jnp.where(mask, 1.0, 0.0).astype(BF)


def dot(a, b, ca=1, cb=0):
    return lax.dot_general(a, b, (((ca,), (cb,)), ((), ())), preferred_element_type=F32)


def pack_body(obs_hbm, tile_hbm, cell_hbm, out_ref, obs_ref, tile_ref, cell_ref, sems):
    copies = [
        pltpu.make_async_copy(src, dst, sems.at[n])
        for n, (src, dst) in enumerate(
            ((tile_hbm, tile_ref), (cell_hbm, cell_ref), (obs_hbm, obs_ref))
        )
    ]
    for copy in copies:
        copy.start()
    before = one(iota((ROWS, ROWS), 0) < iota((ROWS, ROWS), 1))
    for copy in copies:
        copy.wait()
    tile = tile_ref[...]
    cell = cell_ref[...]
    named = iota((TILES, ROWS), 0) == tile
    onehot = one(named)
    counts = dot(onehot, before)
    rank = jnp.sum(jnp.where(named, counts, 0.0), axis=0, keepdims=True).astype(jnp.int32)
    place = one(iota((PACK, ROWS), 0) == tile * SLOT + rank)
    high = (cell >> 5).astype(F32)
    low = (cell & 31).astype(F32)
    lane = iota((CH, ROWS), 0)
    marks = jnp.where(lane == rank, high, 0.0) + jnp.where(lane == rank + CAP, low, 0.0)
    marks = dot(onehot, marks.astype(BF), 1, 1)
    mark_place = one(iota((PACK, TILES), 0) == iota((PACK, TILES), 1) * SLOT + CAP)
    packed = dot(place, obs_ref[...]) + dot(mark_place, marks.astype(BF))
    out_ref[...] = packed.astype(BF)


def add_block(block_ref, store):
    block = block_ref[...]
    rows = block.shape[0]
    q = iota((CH, rows), 1)
    t18 = iota((CH, rows), 0) * SLOT
    marks = dot(one(q == t18 + CAP), block)
    marks = marks.T.astype(BF)
    spread = one((q >= t18) & (q < t18 + SLOT))
    wide = dot(marks[: 2 * CAP], spread)
    qf = iota((CAP, rows), 1).astype(F32)
    within = qf - SLOT * jnp.floor((qf + 0.5) * (1.0 / SLOT))
    mine = within == iota((CAP, rows), 0).astype(F32)
    high = jnp.sum(jnp.where(mine, wide[:CAP], 0.0), axis=0, keepdims=True)
    low = jnp.sum(jnp.where(mine, wide[CAP:], 0.0), axis=0, keepdims=True)
    high = jnp.where(within[:1] > CAP - 0.5, -1.0, high)
    lows = jnp.where(iota((LON, rows), 0).astype(F32) == low, 1.0, 0.0)
    for c in range(0, LAT, 8):
        hot = jnp.concatenate(
            [jnp.where(high == float(i), lows, 0.0).astype(BF) for i in range(c, c + 8)], axis=0
        )
        store(slice(c * LON, (c + 8) * LON), dot(hot, block))


def deposit_first(block_ref, acc_ref):
    def store(rows, part):
        acc_ref[rows] = part

    add_block(block_ref, store)


def deposit_next(block_ref, acc_in, acc_ref):
    def store(rows, part):
        acc_ref[rows] = acc_in[rows] + part

    add_block(block_ref, store)


def deposit_last(
    core_ref, block_ref, acc_in, state_ref, we_ref, mixed_ref, a_ref, on_ref, off_ref,
    mixed_f, a_f,
):
    we = we_ref[...]

    def store(rows, part):
        total = acc_in[rows] + part
        a = total.astype(BF)
        a_ref[rows] = a
        a_f[rows] = total
        mixed = state_ref[rows].astype(F32) + dot(a, we)
        mixed_ref[rows] = mixed.astype(BF)
        mixed_f[rows] = mixed

    add_block(block_ref, store)

    def columns(first):
        return jnp.concatenate(
            [
                jnp.concatenate([f[pl.ds(at, LAT, stride=LON), :] for f in (mixed_f, a_f)], axis=1)
                for at in (first, first + 1)
            ],
            axis=0,
        ).astype(BF)

    core = core_ref[0]
    on_ref[...] = columns((1 - core) * (LON - 2))
    off_ref[...] = columns(core * (LON - 2))


def filter_body(quad_ref, near_ref, m_ref, mt_ref, edge_ref, v_ref):
    quad = quad_ref[...]
    near = near_ref[...]
    near = jnp.concatenate([near] * K, axis=0)
    lane = iota((K * LAT, CH), 1)
    coupling = jnp.zeros((K * LAT, CH), F32)
    for j in range(J):
        coupling += jnp.where(near[:, j : j + 1] == lane, quad[:, j : j + 1], 0.0)
    ahead = iota((LAT, 4 * LAT), 1) - iota((LAT, 4 * LAT), 0)
    row = iota((LAT, 4 * LAT), 0)
    links = {0: ((0, 0), (1, 1)), 1: ((1, 0),), 2: ((2, 4),), 3: ((2, 3), (3, 4))}
    for k in range(K):
        for e in range(4):
            part = jnp.zeros((LAT, 4 * LAT), F32)
            for h, b in links[e]:
                for step in range(3):
                    ok = (ahead == LAT * h + step - 1) & (row + (step - 1) >= 0) & (row + (step - 1) < LAT)
                    o = step * 5 + b
                    part += jnp.where(ok, coupling[k * LAT : (k + 1) * LAT, o : o + 1], 0.0)
            edge_ref[(k * 4 + e) * LAT : (k * 4 + e + 1) * LAT] = part.astype(BF)
    coupling = coupling.astype(BF)

    def column(at):
        edge = at - 96
        step = jnp.where(at < 96, at >> 5, edge >> 2)
        side = edge & 3
        col = jnp.where(at < 96, at & 31, jnp.where(side < 2, side - 2, side + 30))
        return step, jnp.where(at < 108, col, -99)

    step, _ = column(iota((CH, CH), 1))
    for b in range(5):
        v_ref[:, b * CH : (b + 1) * CH] = dot(coupling, one(iota((CH, CH), 0) == step * 5 + b))
    _, col = column(iota((LON, CH), 1))
    masks = [
        jnp.where(col == iota((LON, CH), 0) + (b - 2), 1.0, 0.0) for b in range(5)
    ]

    def one_row(i, _):
        parts = []
        for k in range(K):
            row = v_ref[pl.ds(k * LAT + i, 1), :]
            part = masks[0] * row[:, :CH]
            for b in range(1, 5):
                part += masks[b] * row[:, b * CH : (b + 1) * CH]
            parts.append(part)
        whole = jnp.concatenate(parts, axis=0)
        m_ref[i] = jnp.where(iota((K * LON, CH), 1) < 3 * LON, whole, 0.0).astype(BF)
        whole = jnp.concatenate([whole, jnp.zeros((CH - K * LON, CH), F32)], axis=0)
        mt_ref[i] = whole.T.astype(BF)
        return 0

    lax.fori_loop(0, LAT, one_row, 0)


def own_body(m_ref, mixed_ref, a_ref, cot_ref, basis_ref, bat_ref, acot_ref, xp, ba):
    top = LON + CELLS
    xp[:LON] = jnp.zeros((LON, 2 * CH), BF)
    xp[LON:top, :CH] = mixed_ref[...]
    xp[LON:top, CH:] = a_ref[...]
    xp[top:] = jnp.zeros((3 * LON, 2 * CH), BF)

    def gather(i, _):
        at = pl.multiple_of(i * LON, LON)
        part = dot(m_ref[i], xp[pl.ds(at, CH)])
        for k in range(K):
            rows = slice(k * LON, (k + 1) * LON)
            basis_ref[pl.ds(k * CELLS + at, LON)] = part[rows, :CH]
            ba[pl.ds(at, LON), k * CH : (k + 1) * CH] = part[rows, CH:].astype(BF)
        return 0

    lax.fori_loop(0, LAT, gather, 0, unroll=8)
    for k in range(K):
        for c in range(0, CELLS, 256):
            bat_ref[:, k * CELLS + c : k * CELLS + c + 256] = ba[
                c : c + 256, k * CH : (k + 1) * CH
            ].T
    acot_ref[...] = dot(a_ref[...], cot_ref[...], 0, 0)


def block_body(
    core_ref, off_ref, on_ref, basis_in, bat_ref, acot_ref, edge_ref, mixed_ref, cot_ref, wd_ref,
    basis_ref, out_ref, back_ref, g_ref,
    slope_f, slopes, some_ref,
):
    del basis_in
    even = core_ref[0] == 0
    on, off = on_ref[...], off_ref[...]
    halo = jnp.concatenate([jnp.where(even, off, on), jnp.where(even, on, off)], axis=0)
    from_halo = dot(edge_ref[...], halo)
    for k in range(K):
        for e, at in enumerate((0, 1, LON - 2, LON - 1)):
            rows = pl.ds(k * CELLS + at, LAT, stride=LON)
            n = (k * 4 + e) * LAT
            basis_ref[rows, :] = basis_ref[rows, :] + from_halo[n : n + LAT, :CH]
    wd = wd_ref[...]
    for c in range(0, CELLS, 256):
        rows = slice(c, c + 256)
        some = jnp.concatenate(
            [basis_ref[k * CELLS + c : k * CELLS + c + 256].astype(BF) for k in range(K)], axis=1
        )
        some_ref[rows] = some
        v = dot(some, wd)
        square = v * v
        half = 0.5 + 0.5 * jnp.tanh(v * (tanh_scale + (tanh_scale * cubic_weight) * square))
        out_ref[rows] = (mixed_ref[rows].astype(F32) + v * half).astype(BF)
        rate = half + (v * half) * (1.0 - half) * (
            2.0 * tanh_scale + (6.0 * tanh_scale * cubic_weight) * square
        )
        slope = cot_ref[rows].astype(F32) * rate
        slope_f[rows] = slope
        slope = slope.astype(BF)
        slopes[rows] = slope
        back = dot(slope, wd, 1, 1).astype(BF)
        for k in range(K):
            back_ref[k * CELLS + c : k * CELLS + c + 256] = back[:, k * CH : (k + 1) * CH]
    gd = dot(slopes[...], some_ref[...], 0, 0)
    g_ref[: K * CH] = (gd.T * GRID_SCALE).astype(BF)
    go = acot_ref[...] + dot(bat_ref[...], back_ref[...])
    sides = jnp.concatenate(
        [slope_f[pl.ds(at, LAT, stride=LON), :] for at in (0, 1, LON - 2, LON - 1)], axis=0
    ).astype(BF)
    back = dot(sides, wd, 1, 1).astype(BF)
    for k in range(K):
        some = from_halo[k * 4 * LAT : (k + 1) * 4 * LAT, CH:].astype(BF)
        go += dot(some, back[:, k * CH : (k + 1) * CH], 0, 0)
    g_ref[K * CH :] = (go * OBS_SCALE).astype(BF)


def spread_body(core_ref, mt_ref, back_ref, cot_ref, gs_ref, on_ref, off_ref, tp, h3):
    tp[...] = jnp.zeros((CELLS + 2 * LON, CH), F32)
    none = jnp.zeros((CH - K * LON, CH), BF)

    def scatter(i, _):
        at = pl.multiple_of(i * LON, LON)
        near = [back_ref[pl.ds(k * CELLS + at, LON)] for k in range(K)]
        part = dot(mt_ref[i], jnp.concatenate([*near, none], axis=0))
        tp[pl.ds(at, 3 * LON)] += part[: 3 * LON]
        h3[i] = part[3 * LON : 3 * LON + 16]
        return 0

    lax.fori_loop(0, LAT, scatter, 0, unroll=4)
    gs_ref[...] = cot_ref[...].astype(F32) + tp[LON : LON + CELLS]
    pad = jnp.zeros((1, 16, CH), F32)
    side = jnp.concatenate([pad, h3[...], pad], axis=0)
    side = side[2:, 0:4] + side[1 : LAT + 1, 4:8] + side[:LAT, 8:12]
    even = core_ref[0] == 0
    left, right = side[:, :2], side[:, 2:]
    on_ref[...] = jnp.where(even, right, left)
    off_ref[...] = jnp.where(even, left, right)


def finish_body(core_ref, off_ref, on_ref, gs_ref, out_ref):
    even = core_ref[0] == 0
    on, off = on_ref[...], off_ref[...]
    left, right = jnp.where(even, off, on), jnp.where(even, on, off)
    full = jnp.concatenate([left, jnp.zeros((LAT, LON - 4, CH), F32), right], axis=1)
    out_ref[...] = (gs_ref[...].reshape(LAT, LON, CH) + full).astype(BF)


def sum_body(parts_ref, out_ref):
    total = jnp.sum(parts_ref[...].astype(F32), axis=0, keepdims=True).astype(BF)
    out_ref[...] = jnp.broadcast_to(total.astype(F32), out_ref.shape).astype(BF)


def ending_body(total_ref, disco_ref, obs_ref):
    disco_ref[...] = total_ref[: K * CH].astype(F32)
    obs_ref[...] = total_ref[K * CH :].astype(F32)


def local(
    state, obs_values, obs_tile, obs_cell, neighbours, quadrature, embed_weight, disco_weight,
    cotangent,
):
    exchange = functools.partial(
        lax.all_to_all, axis_name="tile", split_axis=0, concat_axis=0, tiled=True
    )
    core = (lax.axis_index("tile") % 2).reshape(1)
    together = lax.optimization_barrier
    grid_rows = (CELLS, CH)
    cot = cotangent.reshape(grid_rows)
    packed = call(
        pack_body,
        sds((PACK, CH), BF),
        3,
        [
            pltpu.VMEM((ROWS, CH), BF),
            pltpu.VMEM((1, ROWS), jnp.int32),
            pltpu.VMEM((1, ROWS), jnp.int32),
            pltpu.SemaphoreType.DMA((3,)),
        ],
        flops=1 << 28,
        name="pack",
        space=pl.BlockSpec(memory_space=pl.ANY),
        vmem=60,
    )(obs_values, obs_tile.reshape(1, ROWS), obs_cell.reshape(1, ROWS))
    packed, quadrature, neighbours = together((packed, quadrature, neighbours))
    mine = exchange(packed.reshape(TILES, SLOT // 2, 2, CH)).reshape(PACK, CH)
    m, mt, edge = call(
        filter_body,
        (sds((LAT, K * LON, CH), BF), sds((LAT, CH, CH), BF), sds((K * 4 * LAT, 4 * LAT), BF)),
        2,
        [pltpu.VMEM((K * LAT, 5 * CH), F32)],
        flops=1 << 32,
        bytes_accessed=1 << 22,
        name="filters",
    )(quadrature.reshape(K * LAT, J), neighbours)
    mine, m, mt, edge = together((mine, m, mt, edge))

    def pair(x, turn):
        pairs = []
        for tile in range(TILES):
            flip = (1, 0, 3, 2) if (tile + turn) % 2 == 0 else (3, 2, 1, 0)
            pairs += [(tile * 4 + c, tile * 4 + flip[c]) for c in range(4)]
        return lax.ppermute(x, ("tile", "chan"), pairs)

    cost = dict(flops=2 * CELLS * PACK * CH, bytes_accessed=1 << 20)
    first = pair(mine, 0)
    acc = call(deposit_first, sds(grid_rows, F32), 1, name="deposit", **cost)(mine)
    mine, acc = together((mine, acc))
    second = pair(mine, 1)
    across = pair(first, 1)
    for block in (first, second):
        acc = call(deposit_next, sds(grid_rows, F32), 2, name="deposit", **cost)(block, acc)
    mixed, a, on, off = call(
        deposit_last,
        (
            sds(grid_rows, BF),
            sds(grid_rows, BF),
            sds((2 * LAT, 2 * CH), BF),
            sds((2 * LAT, 2 * CH), BF),
        ),
        4,
        [pltpu.VMEM(grid_rows, F32), pltpu.VMEM(grid_rows, F32)],
        flops=1 << 28,
        bytes_accessed=1 << 20,
        name="mix",
        scalars=1,
    )(core, across, acc, state.reshape(grid_rows), embed_weight)

    def swap_on(x):
        return lax.ppermute(x, "tile", [(t, t ^ 1) for t in range(TILES)])

    def swap_off(x):
        return lax.ppermute(
            x, "tile", [(t, (t + 1 if t % 2 else t - 1) % TILES) for t in range(TILES)]
        )

    off, on = swap_off(off), swap_on(on)
    basis, bat, acot = call(
        own_body,
        (sds((K * CELLS, CH), F32), sds((CH, K * CELLS), BF), sds((CH, CH), F32)),
        4,
        [pltpu.VMEM((CELLS + 4 * LON, 2 * CH), BF), pltpu.VMEM((CELLS, K * CH), BF)],
        flops=1 << 31,
        bytes_accessed=1 << 22,
        name="own",
    )(m, mixed, a, cot)
    _, output, back, grads = call(
        block_body,
        (
            sds((K * CELLS, CH), F32),
            sds(grid_rows, BF),
            sds((K * CELLS, CH), BF),
            sds((K * CH + CH, CH), BF),
        ),
        9,
        [
            pltpu.VMEM(grid_rows, F32),
            pltpu.VMEM(grid_rows, BF),
            pltpu.VMEM((CELLS, K * CH), BF),
        ],
        flops=1 << 30,
        bytes_accessed=1 << 22,
        name="block",
        aliases={3: 0},
        scalars=1,
    )(
        core, off, on, basis, bat, acot, edge, mixed, cot, disco_weight.reshape(K * CH, CH)
    )
    parts = exchange(grads.reshape(TILES, 8, CH))
    gs, on, off = call(
        spread_body,
        (sds(grid_rows, F32), sds((LAT, 2, CH), F32), sds((LAT, 2, CH), F32)),
        3,
        [pltpu.VMEM((CELLS + 2 * LON, CH), F32), pltpu.VMEM((LAT, 16, CH), F32)],
        flops=1 << 31,
        bytes_accessed=1 << 22,
        name="spread",
        scalars=1,
    )(core, mt, back, cot)
    parts, gs, on, off = together((parts, gs, on, off))
    off, on = swap_off(off), swap_on(on)
    grad_state = call(
        finish_body, sds((LAT, LON, CH), BF), 3, bytes_accessed=1 << 20, name="finish", scalars=1
    )(core, off, on, gs)
    summed = call(sum_body, sds((TILES, 8, CH), BF), 1, bytes_accessed=1 << 18, name="sum")(parts)
    grad_disco, grad_obs = call(
        ending_body,
        (sds((K * CH, CH), F32), sds((CH, CH), F32)),
        1,
        bytes_accessed=1 << 18,
        name="ending",
    )(exchange(summed).reshape(K * CH + CH, CH))
    return (
        output.reshape(LAT, LON, CH),
        grad_state,
        grad_disco.reshape(K, CH, CH),
        grad_obs,
    )


def solution(mesh):
    in_specs = (
        P(None, "tile", "chan"),
        P(("tile", "chan"), None),
        P(("tile", "chan"), None),
        P(("tile", "chan")),
        P(),
        P(),
        P(None, "chan"),
        P(None, None, "chan"),
        P(None, "tile", "chan"),
    )
    out_specs = (
        P(None, "tile", "chan"),
        P(None, "tile", "chan"),
        P(None, None, "chan"),
        P(None, "chan"),
    )
    return jax.shard_map(local, mesh=mesh, in_specs=in_specs, out_specs=out_specs, check_vma=False)
```

```python
import functools

import jax
import jax.numpy as jnp
from jax import lax
from jax.experimental import pallas as pl
from jax.experimental.pallas import tpu as pltpu
from jax.sharding import PartitionSpec as P

K = 3
J = 8
LAT = 40
LON = 32
CH = 128
CELLS = LAT * LON
ROWS = 512
TILES = 64
CAP = 16
PLANES = [[z * 8 + i for i in range(8)] for z in range(8)]
COLUMNS = [[z * 8 + i for z in range(8)] for i in range(8)]
SLOT = 18
PACK = TILES * SLOT
BF = jnp.bfloat16
F32 = jnp.float32
tanh_scale = 0.7978845608028654
cubic_weight = 0.044715
GRID_SCALE = float(CELLS * TILES) ** -0.5
OBS_SCALE = float(ROWS * TILES * 4) ** -0.5

VM = pl.BlockSpec(memory_space=pltpu.VMEM)
SM = pl.BlockSpec(memory_space=pltpu.SMEM)
HB = pl.BlockSpec(memory_space=pltpu.HBM)


def call(body, outs, n_in, scratch=(), flops=0, bytes_accessed=0, name=None, space=VM, aliases=None, scalars=0, vmem=16, hbm=0):
    return pl.pallas_call(
        body,
        out_shape=outs,
        in_specs=[SM] * scalars + [HB] * hbm + [space] * n_in,
        out_specs=jax.tree.map(lambda _: VM, outs),
        scratch_shapes=list(scratch),
        compiler_params=pltpu.CompilerParams(vmem_limit_bytes=vmem << 20),
        cost_estimate=pl.CostEstimate(
            flops=flops, bytes_accessed=bytes_accessed, transcendentals=0
        ),
        name=name,
        input_output_aliases=aliases or {},
    )


def sds(shape, dtype):
    return jax.ShapeDtypeStruct(shape, dtype)


def iota(shape, dim):
    return lax.broadcasted_iota(jnp.int32, shape, dim)


def one(mask):
    return jnp.where(mask, 1.0, 0.0).astype(BF)


def dot(a, b, ca=1, cb=0):
    return lax.dot_general(a, b, (((ca,), (cb,)), ((), ())), preferred_element_type=F32)


def pack_body(obs_hbm, tile_hbm, cell_hbm, out_ref, obs_ref, tile_ref, cell_ref, sems):
    copies = [
        pltpu.make_async_copy(src, dst, sems.at[n])
        for n, (src, dst) in enumerate(
            ((tile_hbm, tile_ref), (cell_hbm, cell_ref), (obs_hbm, obs_ref))
        )
    ]
    for copy in copies:
        copy.start()
    before = one(iota((ROWS, ROWS), 0) < iota((ROWS, ROWS), 1))
    for copy in copies:
        copy.wait()
    tile = tile_ref[...]
    cell = cell_ref[...]
    named = iota((TILES, ROWS), 0) == tile
    onehot = one(named)
    counts = dot(onehot, before)
    rank = jnp.sum(jnp.where(named, counts, 0.0), axis=0, keepdims=True).astype(jnp.int32)
    place = one(iota((PACK, ROWS), 0) == tile * SLOT + rank)
    high = (cell >> 5).astype(F32)
    low = (cell & 31).astype(F32)
    lane = iota((CH, ROWS), 0)
    marks = jnp.where(lane == rank, high, 0.0) + jnp.where(lane == rank + CAP, low, 0.0)
    marks = dot(onehot, marks.astype(BF), 1, 1)
    mark_place = one(iota((PACK, TILES), 0) == iota((PACK, TILES), 1) * SLOT + CAP)
    packed = dot(place, obs_ref[...]) + dot(mark_place, marks.astype(BF))
    out_ref[...] = packed.astype(BF)


def add_block(block_ref, store):
    block = block_ref[...]
    rows = block.shape[0]
    q = iota((CH, rows), 1)
    t18 = iota((CH, rows), 0) * SLOT
    marks = dot(one(q == t18 + CAP), block)
    marks = marks.T.astype(BF)
    spread = one((q >= t18) & (q < t18 + SLOT))
    wide = dot(marks[: 2 * CAP], spread)
    qf = iota((CAP, rows), 1).astype(F32)
    within = qf - SLOT * jnp.floor((qf + 0.5) * (1.0 / SLOT))
    mine = within == iota((CAP, rows), 0).astype(F32)
    high = jnp.sum(jnp.where(mine, wide[:CAP], 0.0), axis=0, keepdims=True)
    low = jnp.sum(jnp.where(mine, wide[CAP:], 0.0), axis=0, keepdims=True)
    high = jnp.where(within[:1] > CAP - 0.5, -1.0, high)
    lows = jnp.where(iota((LON, rows), 0).astype(F32) == low, 1.0, 0.0)
    for c in range(0, LAT, 8):
        hot = jnp.concatenate(
            [jnp.where(high == float(i), lows, 0.0).astype(BF) for i in range(c, c + 8)], axis=0
        )
        store(slice(c * LON, (c + 8) * LON), dot(hot, block))


def deposit_first(block_ref, acc_ref):
    def store(rows, part):
        acc_ref[rows] = part

    add_block(block_ref, store)


def side_columns(core_ref):
    on = (1 - core_ref[0]) * (LON - 2)
    off = core_ref[0] * (LON - 2)
    return (on, on + 1, off, off + 1)


def take_sides(core_ref, cells_ref, out_ref):
    for n, at in enumerate(side_columns(core_ref)):
        out_ref[n * LAT : (n + 1) * LAT] = cells_ref[pl.ds(at, LAT, stride=LON), :]


def sides_body(core_ref, state_ref, out_ref, wide):
    wide[...] = state_ref[...].astype(F32)
    take_sides(core_ref, wide, out_ref)


def deposit_pair(core_ref, block_ref, acc_in, acc_ref, send_ref, side_ref, side_send_ref):
    def store(rows, part):
        total = acc_in[rows] + part
        acc_ref[rows] = total
        send_ref[rows] = total.astype(BF)

    add_block(block_ref, store)
    take_sides(core_ref, acc_ref, side_ref)
    side_send_ref[...] = side_ref[...].astype(BF)


def edges_body(side_ref, other_ref, state_ref, we_ref, on_ref, off_ref):
    sums = (side_ref[...] + other_ref[...].astype(F32)).astype(BF)
    mixed = (state_ref[...] + dot(sums, we_ref[...])).astype(BF)
    both = jnp.concatenate([mixed, sums], axis=1)
    on_ref[...] = both[: 2 * LAT]
    off_ref[...] = both[2 * LAT :]


def filter_body(quad_ref, near_ref, m_ref, mt_ref, edge_ref, v_ref):
    quad = quad_ref[...]
    near = near_ref[...]
    near = jnp.concatenate([near] * K, axis=0)
    lane = iota((K * LAT, CH), 1)
    coupling = jnp.zeros((K * LAT, CH), F32)
    for j in range(J):
        coupling += jnp.where(near[:, j : j + 1] == lane, quad[:, j : j + 1], 0.0)
    ahead = iota((LAT, 4 * LAT), 1) - iota((LAT, 4 * LAT), 0)
    row = iota((LAT, 4 * LAT), 0)
    parts = []
    links = {0: ((0, 0), (1, 1)), 1: ((1, 0),), 2: ((2, 4),), 3: ((2, 3), (3, 4))}
    for k in range(K):
        for e in range(4):
            part = jnp.zeros((LAT, 4 * LAT), F32)
            for h, b in links[e]:
                for step in range(3):
                    ok = (ahead == LAT * h + step - 1) & (row + (step - 1) >= 0) & (row + (step - 1) < LAT)
                    o = step * 5 + b
                    part += jnp.where(ok, coupling[k * LAT : (k + 1) * LAT, o : o + 1], 0.0)
            parts.append(part)
    edge_ref[...] = jnp.concatenate(parts, axis=0).astype(BF)
    coupling = coupling.astype(BF)

    def column(at):
        edge = at - 96
        step = jnp.where(at < 96, at >> 5, edge >> 2)
        side = edge & 3
        col = jnp.where(at < 96, at & 31, jnp.where(side < 2, side - 2, side + 30))
        return step, jnp.where(at < 108, col, -99)

    step, _ = column(iota((CH, CH), 1))
    for b in range(5):
        v_ref[:, b * CH : (b + 1) * CH] = dot(coupling, one(iota((CH, CH), 0) == step * 5 + b))
    _, col = column(iota((LON, CH), 1))
    masks = [
        jnp.where(col == iota((LON, CH), 0) + (b - 2), 1.0, 0.0) for b in range(5)
    ]

    def one_row(i, _):
        parts = []
        for k in range(K):
            row = v_ref[pl.ds(k * LAT + i, 1), :]
            part = masks[0] * row[:, :CH]
            for b in range(1, 5):
                part += masks[b] * row[:, b * CH : (b + 1) * CH]
            parts.append(part)
        whole = jnp.concatenate(parts, axis=0)
        m_ref[i] = jnp.where(iota((K * LON, CH), 1) < 3 * LON, whole, 0.0).astype(BF)
        whole = jnp.concatenate([whole, jnp.zeros((CH - K * LON, CH), F32)], axis=0)
        mt_ref[i] = whole.T.astype(BF)
        return 0

    lax.fori_loop(0, LAT, one_row, 0, unroll=8)


def own_body(
    m_ref, acc_ref, other_ref, state_ref, we_ref, cot_ref,
    mixed_ref, basis_ref, bat_ref, acot_ref,
    xp, ba,
):
    top = LON + CELLS
    xp[:LON] = jnp.zeros((LON, 2 * CH), BF)
    we = we_ref[...]
    for c in range(0, CELLS, 256):
        rows = slice(c, c + 256)
        a = (acc_ref[rows] + other_ref[rows].astype(F32)).astype(BF)
        mixed = (state_ref[rows].astype(F32) + dot(a, we)).astype(BF)
        mixed_ref[rows] = mixed
        xp[LON + c : LON + c + 256, :CH] = mixed
        xp[LON + c : LON + c + 256, CH:] = a
    xp[top:] = jnp.zeros((3 * LON, 2 * CH), BF)

    def gather(i, _):
        at = pl.multiple_of(i * LON, LON)
        part = dot(m_ref[i], xp[pl.ds(at, CH)])
        for k in range(K):
            rows = slice(k * LON, (k + 1) * LON)
            basis_ref[pl.ds(k * CELLS + at, LON)] = part[rows, :CH]
            ba[pl.ds(at, LON), k * CH : (k + 1) * CH] = part[rows, CH:].astype(BF)
        return 0

    lax.fori_loop(0, LAT, gather, 0, unroll=8)
    for k in range(K):
        for c in range(0, CELLS, 256):
            bat_ref[:, k * CELLS + c : k * CELLS + c + 256] = ba[
                c : c + 256, k * CH : (k + 1) * CH
            ].T
    acot_ref[...] = dot(xp[LON:top, CH:], cot_ref[...], 0, 0)


def block_body(
    core_ref, off_ref, on_ref, basis_in, bat_ref, acot_ref, edge_ref, mixed_ref, cot_ref, wd_ref,
    basis_ref, out_ref, back_ref, g_ref,
    slope_f, slopes, some_ref,
):
    del basis_in
    even = core_ref[0] == 0
    on, off = on_ref[...], off_ref[...]
    halo = jnp.concatenate([jnp.where(even, off, on), jnp.where(even, on, off)], axis=0)
    from_halo = dot(edge_ref[...], halo)
    for k in range(K):
        for e, at in enumerate((0, 1, LON - 2, LON - 1)):
            rows = pl.ds(k * CELLS + at, LAT, stride=LON)
            n = (k * 4 + e) * LAT
            basis_ref[rows, :] = basis_ref[rows, :] + from_halo[n : n + LAT, :CH]
    wd = wd_ref[...]
    for c in range(0, CELLS, 256):
        rows = slice(c, c + 256)
        some = jnp.concatenate(
            [basis_ref[k * CELLS + c : k * CELLS + c + 256].astype(BF) for k in range(K)], axis=1
        )
        some_ref[rows] = some
        v = dot(some, wd)
        square = v * v
        half = 0.5 + 0.5 * jnp.tanh(v * (tanh_scale + (tanh_scale * cubic_weight) * square))
        out_ref[rows] = (mixed_ref[rows].astype(F32) + v * half).astype(BF)
        rate = half + (v * half) * (1.0 - half) * (
            2.0 * tanh_scale + (6.0 * tanh_scale * cubic_weight) * square
        )
        slope = cot_ref[rows].astype(F32) * rate
        slope_f[rows] = slope
        slope = slope.astype(BF)
        slopes[rows] = slope
        back = dot(slope, wd, 1, 1).astype(BF)
        for k in range(K):
            back_ref[k * CELLS + c : k * CELLS + c + 256] = back[:, k * CH : (k + 1) * CH]
    gd = dot(slopes[...], some_ref[...], 0, 0)
    g_ref[: K * CH] = (gd.T * GRID_SCALE).astype(BF)
    go = acot_ref[...] + dot(bat_ref[...], back_ref[...])
    sides = jnp.concatenate(
        [slope_f[pl.ds(at, LAT, stride=LON), :] for at in (0, 1, LON - 2, LON - 1)], axis=0
    ).astype(BF)
    back = dot(sides, wd, 1, 1).astype(BF)
    for k in range(K):
        some = from_halo[k * 4 * LAT : (k + 1) * 4 * LAT, CH:].astype(BF)
        go += dot(some, back[:, k * CH : (k + 1) * CH], 0, 0)
    g_ref[K * CH :] = (go * OBS_SCALE).astype(BF)


def spread_body(core_ref, mt_hbm, back_ref, cot_ref, gs_ref, on_ref, off_ref, tp, h3, mt_ref, sems):
    step = LAT // 5
    copies = [
        pltpu.make_async_copy(
            mt_hbm.at[c * step : (c + 1) * step], mt_ref.at[c * step : (c + 1) * step], sems.at[c]
        )
        for c in range(5)
    ]
    for copy in copies:
        copy.start()
    tp[...] = jnp.zeros((CELLS + 2 * LON, CH), F32)
    none = jnp.zeros((CH - K * LON, CH), BF)

    def scatter(i, _):
        at = pl.multiple_of(i * LON, LON)
        near = [back_ref[pl.ds(k * CELLS + at, LON)] for k in range(K)]
        part = dot(mt_ref[i], jnp.concatenate([*near, none], axis=0))
        tp[pl.ds(at, 3 * LON)] += part[: 3 * LON]
        h3[i] = part[3 * LON : 3 * LON + 16]
        return 0

    for c, copy in enumerate(copies):
        copy.wait()
        lax.fori_loop(c * step, (c + 1) * step, scatter, 0, unroll=8)
    gs_ref[...] = cot_ref[...].astype(F32) + tp[LON : LON + CELLS]
    pad = jnp.zeros((1, 16, CH), F32)
    side = jnp.concatenate([pad, h3[...], pad], axis=0)
    side = side[2:, 0:4] + side[1 : LAT + 1, 4:8] + side[:LAT, 8:12]
    even = core_ref[0] == 0
    left, right = side[:, :2], side[:, 2:]
    on_ref[...] = jnp.where(even, right, left)
    off_ref[...] = jnp.where(even, left, right)


def finish_body(core_ref, off_ref, on_ref, gs_ref, out_ref):
    even = core_ref[0] == 0
    on, off = on_ref[...], off_ref[...]
    left, right = jnp.where(even, off, on), jnp.where(even, on, off)
    full = jnp.concatenate([left, jnp.zeros((LAT, LON - 4, CH), F32), right], axis=1)
    out_ref[...] = (gs_ref[...].reshape(LAT, LON, CH) + full).astype(BF)


def sum_body(parts_ref, out_ref):
    total = jnp.sum(parts_ref[...].astype(F32), axis=0, keepdims=True).astype(BF)
    out_ref[...] = jnp.broadcast_to(total.astype(F32), out_ref.shape).astype(BF)


def ending_body(total_ref, disco_ref, obs_ref):
    disco_ref[...] = total_ref[: K * CH].astype(F32)
    obs_ref[...] = total_ref[K * CH :].astype(F32)


def local(
    state, obs_values, obs_tile, obs_cell, neighbours, quadrature, embed_weight, disco_weight,
    cotangent,
):
    exchange = functools.partial(
        lax.all_to_all, axis_name="tile", split_axis=0, concat_axis=0, tiled=True
    )
    plane = functools.partial(exchange, axis_index_groups=PLANES)
    column = functools.partial(exchange, axis_index_groups=COLUMNS)
    core = (lax.axis_index("tile") % 2).reshape(1)
    together = lax.optimization_barrier
    grid_rows = (CELLS, CH)
    cot = cotangent.reshape(grid_rows)
    packed = call(
        pack_body,
        sds((PACK, CH), BF),
        3,
        [
            pltpu.VMEM((ROWS, CH), BF),
            pltpu.VMEM((1, ROWS), jnp.int32),
            pltpu.VMEM((1, ROWS), jnp.int32),
            pltpu.SemaphoreType.DMA((3,)),
        ],
        flops=1 << 28,
        name="pack",
        space=HB,
        vmem=60,
    )(obs_values, obs_tile.reshape(1, ROWS), obs_cell.reshape(1, ROWS))
    packed, quadrature, neighbours, state = together((packed, quadrature, neighbours, state))
    state = state.reshape(grid_rows)
    mine = exchange(packed.reshape(TILES, SLOT // 2, 2, CH)).reshape(PACK, CH)
    sides = call(
        sides_body,
        sds((4 * LAT, CH), F32),
        1,
        [pltpu.VMEM(grid_rows, F32)],
        flops=1 << 28,
        name="sides",
        scalars=1,
    )(core, state)
    m, mt, edge = call(
        filter_body,
        (sds((LAT, K * LON, CH), BF), sds((LAT, CH, CH), BF), sds((K * 4 * LAT, 4 * LAT), BF)),
        2,
        [pltpu.VMEM((K * LAT, 5 * CH), F32)],
        flops=1 << 32,
        bytes_accessed=1 << 22,
        name="filters",
    )(quadrature.reshape(K * LAT, J), neighbours)
    mine, m, mt, edge, sides = together((mine, m, mt, edge, sides))

    def pair(x, turn):
        pairs = []
        for tile in range(TILES):
            flip = (1, 0, 3, 2) if (tile + turn) % 2 == 0 else (3, 2, 1, 0)
            pairs += [(tile * 4 + c, tile * 4 + flip[c]) for c in range(4)]
        return lax.ppermute(x, ("tile", "chan"), pairs)

    cost = dict(flops=2 * CELLS * PACK * CH, bytes_accessed=1 << 20)
    first = pair(mine, 0)
    acc = call(deposit_first, sds(grid_rows, F32), 1, name="deposit", **cost)(mine)
    acc, send, side, side_send = call(
        deposit_pair,
        (
            sds(grid_rows, F32),
            sds(grid_rows, BF),
            sds((4 * LAT, CH), F32),
            sds((4 * LAT, CH), BF),
        ),
        2,
        name="deposit_pair",
        scalars=1,
        **cost,
    )(core, first, acc)
    other_side = pair(side_send, 1)
    other = pair(send, 1)
    on, off = call(
        edges_body,
        (sds((2 * LAT, 2 * CH), BF), sds((2 * LAT, 2 * CH), BF)),
        4,
        flops=1 << 28,
        bytes_accessed=1 << 20,
        name="edges",
    )(side, other_side, sides, embed_weight)

    def swap_on(x):
        return lax.ppermute(x, "tile", [(t, t ^ 1) for t in range(TILES)])

    def swap_off(x):
        return lax.ppermute(
            x, "tile", [(t, (t + 1 if t % 2 else t - 1) % TILES) for t in range(TILES)]
        )

    off, on = swap_off(off), swap_on(on)
    mixed, basis, bat, acot = call(
        own_body,
        (
            sds(grid_rows, BF),
            sds((K * CELLS, CH), F32),
            sds((CH, K * CELLS), BF),
            sds((CH, CH), F32),
        ),
        6,
        [pltpu.VMEM((CELLS + 4 * LON, 2 * CH), BF), pltpu.VMEM((CELLS, K * CH), BF)],
        flops=1 << 31,
        bytes_accessed=1 << 22,
        name="own",
    )(m, acc, other, state, embed_weight, cot)
    _, output, back, grads = call(
        block_body,
        (
            sds((K * CELLS, CH), F32),
            sds(grid_rows, BF),
            sds((K * CELLS, CH), BF),
            sds((K * CH + CH, CH), BF),
        ),
        9,
        [
            pltpu.VMEM(grid_rows, F32),
            pltpu.VMEM(grid_rows, BF),
            pltpu.VMEM((CELLS, K * CH), BF),
        ],
        flops=1 << 30,
        bytes_accessed=1 << 22,
        name="block",
        aliases={3: 0},
        scalars=1,
    )(
        core, off, on, basis, bat, acot, edge, mixed, cot, disco_weight.reshape(K * CH, CH)
    )
    parts = plane(grads.reshape(8, 64, CH))
    gs, on, off = call(
        spread_body,
        (sds(grid_rows, F32), sds((LAT, 2, CH), F32), sds((LAT, 2, CH), F32)),
        2,
        [
            pltpu.VMEM((CELLS + 2 * LON, CH), F32),
            pltpu.VMEM((LAT, 16, CH), F32),
            pltpu.VMEM((LAT, CH, CH), BF),
            pltpu.SemaphoreType.DMA((5,)),
        ],
        flops=1 << 31,
        bytes_accessed=1 << 22,
        name="spread",
        scalars=1,
        hbm=1,
    )(core, mt, back, cot)
    parts, gs, on, off = together((parts, gs, on, off))
    def sum_up(parts):
        return call(sum_body, sds((8, 64, CH), BF), 1, bytes_accessed=1 << 18, name="sum")(parts)

    summed, on, off = together((sum_up(parts), on, off))
    parts = column(summed)
    off, on = swap_off(off), swap_on(on)
    grad_state = call(
        finish_body, sds((LAT, LON, CH), BF), 3, bytes_accessed=1 << 20, name="finish", scalars=1
    )(core, off, on, gs)
    parts, grad_state = together((parts, grad_state))
    grad_disco, grad_obs = call(
        ending_body,
        (sds((K * CH, CH), F32), sds((CH, CH), F32)),
        1,
        bytes_accessed=1 << 18,
        name="ending",
    )(plane(sum_up(parts)).reshape(K * CH + CH, CH))
    return (
        output.reshape(LAT, LON, CH),
        grad_state,
        grad_disco.reshape(K, CH, CH),
        grad_obs,
    )


def solution(mesh):
    in_specs = (
        P(None, "tile", "chan"),
        P(("tile", "chan"), None),
        P(("tile", "chan"), None),
        P(("tile", "chan")),
        P(),
        P(),
        P(None, "chan"),
        P(None, None, "chan"),
        P(None, "tile", "chan"),
    )
    out_specs = (
        P(None, "tile", "chan"),
        P(None, "tile", "chan"),
        P(None, None, "chan"),
        P(None, "chan"),
    )
    return jax.shard_map(local, mesh=mesh, in_specs=in_specs, out_specs=out_specs, check_vma=False)
```

```python
import functools

import jax
import jax.numpy as jnp
from jax import lax
from jax.experimental import pallas as pl
from jax.experimental.pallas import tpu as pltpu
from jax.sharding import PartitionSpec as P

K = 3
J = 8
LAT = 40
LON = 32
CH = 128
CELLS = LAT * LON
ROWS = 512
TILES = 64
CAP = 16
PLANES = [[z * 8 + i for i in range(8)] for z in range(8)]
COLUMNS = [[z * 8 + i for z in range(8)] for i in range(8)]
SLOT = 18
PACK = TILES * SLOT
BF = jnp.bfloat16
F32 = jnp.float32
tanh_scale = 0.7978845608028654
cubic_weight = 0.044715
GRID_SCALE = float(CELLS * TILES) ** -0.5
OBS_SCALE = float(ROWS * TILES * 4) ** -0.5

VM = pl.BlockSpec(memory_space=pltpu.VMEM)
SM = pl.BlockSpec(memory_space=pltpu.SMEM)
HB = pl.BlockSpec(memory_space=pltpu.HBM)


def call(body, outs, n_in, scratch=(), flops=0, bytes_accessed=0, name=None, space=VM, aliases=None, scalars=0, vmem=16, hbm=0):
    return pl.pallas_call(
        body,
        out_shape=outs,
        in_specs=[SM] * scalars + [HB] * hbm + [space] * n_in,
        out_specs=jax.tree.map(lambda _: VM, outs),
        scratch_shapes=list(scratch),
        compiler_params=pltpu.CompilerParams(vmem_limit_bytes=vmem << 20),
        cost_estimate=pl.CostEstimate(
            flops=flops, bytes_accessed=bytes_accessed, transcendentals=0
        ),
        name=name,
        input_output_aliases=aliases or {},
    )


def sds(shape, dtype):
    return jax.ShapeDtypeStruct(shape, dtype)


def iota(shape, dim):
    return lax.broadcasted_iota(jnp.int32, shape, dim)


def one(mask):
    return jnp.where(mask, 1.0, 0.0).astype(BF)


def dot(a, b, ca=1, cb=0):
    return lax.dot_general(a, b, (((ca,), (cb,)), ((), ())), preferred_element_type=F32)


def pack_body(obs_hbm, tile_hbm, cell_hbm, out_ref, obs_ref, tile_ref, cell_ref, sems):
    copies = [
        pltpu.make_async_copy(src, dst, sems.at[n])
        for n, (src, dst) in enumerate(
            ((tile_hbm, tile_ref), (cell_hbm, cell_ref), (obs_hbm, obs_ref))
        )
    ]
    for copy in copies:
        copy.start()
    before = one(iota((ROWS, ROWS), 0) < iota((ROWS, ROWS), 1))
    for copy in copies:
        copy.wait()
    tile = tile_ref[...]
    cell = cell_ref[...]
    named = iota((TILES, ROWS), 0) == tile
    onehot = one(named)
    counts = dot(onehot, before)
    rank = jnp.sum(jnp.where(named, counts, 0.0), axis=0, keepdims=True).astype(jnp.int32)
    place = one(iota((PACK, ROWS), 0) == tile * SLOT + rank)
    high = (cell >> 5).astype(F32)
    low = (cell & 31).astype(F32)
    lane = iota((CH, ROWS), 0)
    marks = jnp.where(lane == rank, high, 0.0) + jnp.where(lane == rank + CAP, low, 0.0)
    marks = dot(onehot, marks.astype(BF), 1, 1)
    mark_place = one(iota((PACK, TILES), 0) == iota((PACK, TILES), 1) * SLOT + CAP)
    packed = dot(place, obs_ref[...]) + dot(mark_place, marks.astype(BF))
    out_ref[...] = packed.astype(BF)


def add_block(block_ref, store):
    block = block_ref[...]
    rows = block.shape[0]
    q = iota((CH, rows), 1)
    t18 = iota((CH, rows), 0) * SLOT
    marks = dot(one(q == t18 + CAP), block)
    marks = marks.T.astype(BF)
    spread = one((q >= t18) & (q < t18 + SLOT))
    wide = dot(marks[: 2 * CAP], spread)
    qf = iota((CAP, rows), 1).astype(F32)
    within = qf - SLOT * jnp.floor((qf + 0.5) * (1.0 / SLOT))
    mine = within == iota((CAP, rows), 0).astype(F32)
    high = jnp.sum(jnp.where(mine, wide[:CAP], 0.0), axis=0, keepdims=True)
    low = jnp.sum(jnp.where(mine, wide[CAP:], 0.0), axis=0, keepdims=True)
    high = jnp.where(within[:1] > CAP - 0.5, -1.0, high)
    lows = jnp.where(iota((LON, rows), 0).astype(F32) == low, 1.0, 0.0)
    for c in range(0, LAT, 8):
        hot = jnp.concatenate(
            [jnp.where(high == float(i), lows, 0.0).astype(BF) for i in range(c, c + 8)], axis=0
        )
        store(slice(c * LON, (c + 8) * LON), dot(hot, block))


def deposit_first(block_ref, acc_ref):
    def store(rows, part):
        acc_ref[rows] = part

    add_block(block_ref, store)


def side_columns(core_ref):
    on = (1 - core_ref[0]) * (LON - 2)
    off = core_ref[0] * (LON - 2)
    return (on, on + 1, off, off + 1)


def take_sides(core_ref, cells_ref, out_ref):
    for n, at in enumerate(side_columns(core_ref)):
        out_ref[n * LAT : (n + 1) * LAT] = cells_ref[pl.ds(at, LAT, stride=LON), :]


def sides_body(core_ref, state_ref, out_ref, wide):
    wide[...] = state_ref[...].astype(F32)
    take_sides(core_ref, wide, out_ref)


def deposit_pair(core_ref, block_ref, acc_in, acc_ref, send_ref, side_ref, side_send_ref):
    def store(rows, part):
        total = acc_in[rows] + part
        acc_ref[rows] = total
        send_ref[rows] = total.astype(BF)

    add_block(block_ref, store)
    take_sides(core_ref, acc_ref, side_ref)
    side_send_ref[...] = side_ref[...].astype(BF)


def edges_body(side_ref, other_ref, state_ref, we_ref, on_ref, off_ref):
    sums = (side_ref[...] + other_ref[...].astype(F32)).astype(BF)
    mixed = (state_ref[...] + dot(sums, we_ref[...])).astype(BF)
    both = jnp.concatenate([mixed, sums], axis=1)
    on_ref[...] = both[: 2 * LAT]
    off_ref[...] = both[2 * LAT :]


def filter_body(quad_ref, near_ref, m_ref, mt_ref, edge_ref, v_ref):
    quad = quad_ref[...]
    near = near_ref[...]
    near = jnp.concatenate([near] * K, axis=0)
    lane = iota((K * LAT, CH), 1)
    coupling = jnp.zeros((K * LAT, CH), F32)
    for j in range(J):
        coupling += jnp.where(near[:, j : j + 1] == lane, quad[:, j : j + 1], 0.0)
    ahead = iota((LAT, 4 * LAT), 1) - iota((LAT, 4 * LAT), 0)
    row = iota((LAT, 4 * LAT), 0)
    parts = []
    links = {0: ((0, 0), (1, 1)), 1: ((1, 0),), 2: ((2, 4),), 3: ((2, 3), (3, 4))}
    for k in range(K):
        for e in range(4):
            part = jnp.zeros((LAT, 4 * LAT), F32)
            for h, b in links[e]:
                for step in range(3):
                    ok = (ahead == LAT * h + step - 1) & (row + (step - 1) >= 0) & (row + (step - 1) < LAT)
                    o = step * 5 + b
                    part += jnp.where(ok, coupling[k * LAT : (k + 1) * LAT, o : o + 1], 0.0)
            parts.append(part)
    edge_ref[...] = jnp.concatenate(parts, axis=0).astype(BF)
    coupling = coupling.astype(BF)

    def column(at):
        edge = at - 96
        step = jnp.where(at < 96, at >> 5, edge >> 2)
        side = edge & 3
        col = jnp.where(at < 96, at & 31, jnp.where(side < 2, side - 2, side + 30))
        return step, jnp.where(at < 108, col, -99)

    step, _ = column(iota((CH, CH), 1))
    for b in range(5):
        v_ref[:, b * CH : (b + 1) * CH] = dot(coupling, one(iota((CH, CH), 0) == step * 5 + b))
    _, col = column(iota((LON, CH), 1))
    masks = [
        jnp.where(col == iota((LON, CH), 0) + (b - 2), 1.0, 0.0) for b in range(5)
    ]

    def one_row(i, _):
        parts = []
        for k in range(K):
            row = v_ref[pl.ds(k * LAT + i, 1), :]
            part = masks[0] * row[:, :CH]
            for b in range(1, 5):
                part += masks[b] * row[:, b * CH : (b + 1) * CH]
            parts.append(part)
        whole = jnp.concatenate(parts, axis=0)
        m_ref[i] = jnp.where(iota((K * LON, CH), 1) < 3 * LON, whole, 0.0).astype(BF)
        whole = jnp.concatenate([whole, jnp.zeros((CH - K * LON, CH), F32)], axis=0)
        mt_ref[i] = whole.T.astype(BF)
        return 0

    lax.fori_loop(0, LAT, one_row, 0, unroll=8)


def own_body(
    m_ref, acc_ref, other_ref, state_ref, we_ref, cot_ref,
    mixed_ref, basis_ref, bat_ref, acot_ref,
    xp, ba,
):
    top = LON + CELLS
    xp[:LON] = jnp.zeros((LON, 2 * CH), BF)
    we = we_ref[...]
    for c in range(0, CELLS, 256):
        rows = slice(c, c + 256)
        a = (acc_ref[rows] + other_ref[rows].astype(F32)).astype(BF)
        mixed = (state_ref[rows].astype(F32) + dot(a, we)).astype(BF)
        mixed_ref[rows] = mixed
        xp[LON + c : LON + c + 256, :CH] = mixed
        xp[LON + c : LON + c + 256, CH:] = a
    xp[top:] = jnp.zeros((3 * LON, 2 * CH), BF)

    def gather(i, _):
        at = pl.multiple_of(i * LON, LON)
        part = dot(m_ref[i], xp[pl.ds(at, CH)])
        for k in range(K):
            rows = slice(k * LON, (k + 1) * LON)
            basis_ref[pl.ds(k * CELLS + at, LON)] = part[rows, :CH]
            ba[pl.ds(at, LON), k * CH : (k + 1) * CH] = part[rows, CH:].astype(BF)
        return 0

    lax.fori_loop(0, LAT, gather, 0, unroll=40)
    for k in range(K):
        for c in range(0, CELLS, 256):
            bat_ref[:, k * CELLS + c : k * CELLS + c + 256] = ba[
                c : c + 256, k * CH : (k + 1) * CH
            ].T
    acot_ref[...] = dot(xp[LON:top, CH:], cot_ref[...], 0, 0)


def block_body(
    core_ref, off_ref, on_ref, basis_in, bat_ref, acot_ref, edge_ref, mixed_ref, cot_ref, wd_ref,
    basis_ref, out_ref, back_ref, g_ref,
    slope_f, slopes, some_ref,
):
    del basis_in
    even = core_ref[0] == 0
    on, off = on_ref[...], off_ref[...]
    halo = jnp.concatenate([jnp.where(even, off, on), jnp.where(even, on, off)], axis=0)
    from_halo = dot(edge_ref[...], halo)
    for k in range(K):
        for e, at in enumerate((0, 1, LON - 2, LON - 1)):
            rows = pl.ds(k * CELLS + at, LAT, stride=LON)
            n = (k * 4 + e) * LAT
            basis_ref[rows, :] = basis_ref[rows, :] + from_halo[n : n + LAT, :CH]
    wd = wd_ref[...]
    for c in range(0, CELLS, 256):
        rows = slice(c, c + 256)
        some = jnp.concatenate(
            [basis_ref[k * CELLS + c : k * CELLS + c + 256].astype(BF) for k in range(K)], axis=1
        )
        some_ref[rows] = some
        v = dot(some, wd)
        square = v * v
        half = 0.5 + 0.5 * jnp.tanh(v * (tanh_scale + (tanh_scale * cubic_weight) * square))
        out_ref[rows] = (mixed_ref[rows].astype(F32) + v * half).astype(BF)
        rate = half + (v * half) * (1.0 - half) * (
            2.0 * tanh_scale + (6.0 * tanh_scale * cubic_weight) * square
        )
        slope = cot_ref[rows].astype(F32) * rate
        slope_f[rows] = slope
        slope = slope.astype(BF)
        slopes[rows] = slope
        back = dot(slope, wd, 1, 1).astype(BF)
        for k in range(K):
            back_ref[k * CELLS + c : k * CELLS + c + 256] = back[:, k * CH : (k + 1) * CH]
    gd = dot(slopes[...], some_ref[...], 0, 0)
    g_ref[: K * CH] = (gd.T * GRID_SCALE).astype(BF)
    go = acot_ref[...] + dot(bat_ref[...], back_ref[...])
    sides = jnp.concatenate(
        [slope_f[pl.ds(at, LAT, stride=LON), :] for at in (0, 1, LON - 2, LON - 1)], axis=0
    ).astype(BF)
    back = dot(sides, wd, 1, 1).astype(BF)
    for k in range(K):
        some = from_halo[k * 4 * LAT : (k + 1) * 4 * LAT, CH:].astype(BF)
        go += dot(some, back[:, k * CH : (k + 1) * CH], 0, 0)
    g_ref[K * CH :] = (go * OBS_SCALE).astype(BF)


def spread_body(core_ref, mt_hbm, back_ref, cot_ref, gs_ref, on_ref, off_ref, tp, h3, mt_ref, sems):
    step = LAT // 5
    copies = [
        pltpu.make_async_copy(
            mt_hbm.at[c * step : (c + 1) * step], mt_ref.at[c * step : (c + 1) * step], sems.at[c]
        )
        for c in range(5)
    ]
    for copy in copies:
        copy.start()
    tp[...] = jnp.zeros((CELLS + 2 * LON, CH), F32)
    none = jnp.zeros((CH - K * LON, CH), BF)

    def scatter(i, _):
        at = pl.multiple_of(i * LON, LON)
        near = [back_ref[pl.ds(k * CELLS + at, LON)] for k in range(K)]
        part = dot(mt_ref[i], jnp.concatenate([*near, none], axis=0))
        tp[pl.ds(at, 3 * LON)] += part[: 3 * LON]
        h3[i] = part[3 * LON : 3 * LON + 16]
        return 0

    for c, copy in enumerate(copies):
        copy.wait()
        lax.fori_loop(c * step, (c + 1) * step, scatter, 0, unroll=8)
    gs_ref[...] = cot_ref[...].astype(F32) + tp[LON : LON + CELLS]
    pad = jnp.zeros((1, 16, CH), F32)
    side = jnp.concatenate([pad, h3[...], pad], axis=0)
    side = side[2:, 0:4] + side[1 : LAT + 1, 4:8] + side[:LAT, 8:12]
    even = core_ref[0] == 0
    left, right = side[:, :2], side[:, 2:]
    on_ref[...] = jnp.where(even, right, left)
    off_ref[...] = jnp.where(even, left, right)


def finish_body(core_ref, off_ref, on_ref, gs_ref, out_ref):
    even = core_ref[0] == 0
    on, off = on_ref[...], off_ref[...]
    left, right = jnp.where(even, off, on), jnp.where(even, on, off)
    full = jnp.concatenate([left, jnp.zeros((LAT, LON - 4, CH), F32), right], axis=1)
    out_ref[...] = (gs_ref[...].reshape(LAT, LON, CH) + full).astype(BF)


def sum_body(parts_ref, out_ref):
    total = jnp.sum(parts_ref[...].astype(F32), axis=0, keepdims=True).astype(BF)
    out_ref[...] = jnp.broadcast_to(total.astype(F32), out_ref.shape).astype(BF)


def ending_body(total_ref, disco_ref, obs_ref):
    disco_ref[...] = total_ref[: K * CH].astype(F32)
    obs_ref[...] = total_ref[K * CH :].astype(F32)


def local(
    state, obs_values, obs_tile, obs_cell, neighbours, quadrature, embed_weight, disco_weight,
    cotangent,
):
    exchange = functools.partial(
        lax.all_to_all, axis_name="tile", split_axis=0, concat_axis=0, tiled=True
    )
    plane = functools.partial(exchange, axis_index_groups=PLANES)
    column = functools.partial(exchange, axis_index_groups=COLUMNS)
    core = (lax.axis_index("tile") % 2).reshape(1)
    together = lax.optimization_barrier
    grid_rows = (CELLS, CH)
    cot = cotangent.reshape(grid_rows)
    packed = call(
        pack_body,
        sds((PACK, CH), BF),
        3,
        [
            pltpu.VMEM((ROWS, CH), BF),
            pltpu.VMEM((1, ROWS), jnp.int32),
            pltpu.VMEM((1, ROWS), jnp.int32),
            pltpu.SemaphoreType.DMA((3,)),
        ],
        flops=1 << 28,
        name="pack",
        space=HB,
        vmem=60,
    )(obs_values, obs_tile.reshape(1, ROWS), obs_cell.reshape(1, ROWS))
    packed, quadrature, neighbours, state = together((packed, quadrature, neighbours, state))
    state = state.reshape(grid_rows)
    mine = exchange(packed.reshape(TILES, SLOT // 2, 2, CH)).reshape(PACK, CH)
    sides = call(
        sides_body,
        sds((4 * LAT, CH), F32),
        1,
        [pltpu.VMEM(grid_rows, F32)],
        flops=1 << 28,
        name="sides",
        scalars=1,
    )(core, state)
    m, mt, edge = call(
        filter_body,
        (sds((LAT, K * LON, CH), BF), sds((LAT, CH, CH), BF), sds((K * 4 * LAT, 4 * LAT), BF)),
        2,
        [pltpu.VMEM((K * LAT, 5 * CH), F32)],
        flops=1 << 32,
        bytes_accessed=1 << 22,
        name="filters",
    )(quadrature.reshape(K * LAT, J), neighbours)
    mine, m, mt, edge, sides = together((mine, m, mt, edge, sides))

    def pair(x, turn):
        pairs = []
        for tile in range(TILES):
            flip = (1, 0, 3, 2) if (tile + turn) % 2 == 0 else (3, 2, 1, 0)
            pairs += [(tile * 4 + c, tile * 4 + flip[c]) for c in range(4)]
        return lax.ppermute(x, ("tile", "chan"), pairs)

    cost = dict(flops=2 * CELLS * PACK * CH, bytes_accessed=1 << 20)
    first = pair(mine, 0)
    acc = call(deposit_first, sds(grid_rows, F32), 1, name="deposit", **cost)(mine)
    acc, send, side, side_send = call(
        deposit_pair,
        (
            sds(grid_rows, F32),
            sds(grid_rows, BF),
            sds((4 * LAT, CH), F32),
            sds((4 * LAT, CH), BF),
        ),
        2,
        name="deposit_pair",
        scalars=1,
        **cost,
    )(core, first, acc)
    other_side = pair(side_send, 1)
    send, other_side = together((send, other_side))
    other = pair(send, 1)
    on, off = call(
        edges_body,
        (sds((2 * LAT, 2 * CH), BF), sds((2 * LAT, 2 * CH), BF)),
        4,
        flops=1 << 28,
        bytes_accessed=1 << 20,
        name="edges",
    )(side, other_side, sides, embed_weight)

    def swap_on(x):
        return lax.ppermute(x, "tile", [(t, t ^ 1) for t in range(TILES)])

    def swap_off(x):
        return lax.ppermute(
            x, "tile", [(t, (t + 1 if t % 2 else t - 1) % TILES) for t in range(TILES)]
        )

    off, on = swap_off(off), swap_on(on)
    mixed, basis, bat, acot = call(
        own_body,
        (
            sds(grid_rows, BF),
            sds((K * CELLS, CH), F32),
            sds((CH, K * CELLS), BF),
            sds((CH, CH), F32),
        ),
        6,
        [pltpu.VMEM((CELLS + 4 * LON, 2 * CH), BF), pltpu.VMEM((CELLS, K * CH), BF)],
        flops=1 << 31,
        bytes_accessed=1 << 22,
        name="own",
    )(m, acc, other, state, embed_weight, cot)
    _, output, back, grads = call(
        block_body,
        (
            sds((K * CELLS, CH), F32),
            sds(grid_rows, BF),
            sds((K * CELLS, CH), BF),
            sds((K * CH + CH, CH), BF),
        ),
        9,
        [
            pltpu.VMEM(grid_rows, F32),
            pltpu.VMEM(grid_rows, BF),
            pltpu.VMEM((CELLS, K * CH), BF),
        ],
        flops=1 << 30,
        bytes_accessed=1 << 22,
        name="block",
        aliases={3: 0},
        scalars=1,
    )(
        core, off, on, basis, bat, acot, edge, mixed, cot, disco_weight.reshape(K * CH, CH)
    )
    parts = plane(grads.reshape(8, 64, CH))
    gs, on, off = call(
        spread_body,
        (sds(grid_rows, F32), sds((LAT, 2, CH), F32), sds((LAT, 2, CH), F32)),
        2,
        [
            pltpu.VMEM((CELLS + 2 * LON, CH), F32),
            pltpu.VMEM((LAT, 16, CH), F32),
            pltpu.VMEM((LAT, CH, CH), BF),
            pltpu.SemaphoreType.DMA((5,)),
        ],
        flops=1 << 31,
        bytes_accessed=1 << 22,
        name="spread",
        scalars=1,
        hbm=1,
    )(core, mt, back, cot)
    parts, gs, on, off = together((parts, gs, on, off))
    def sum_up(parts):
        return call(sum_body, sds((8, 64, CH), BF), 1, bytes_accessed=1 << 18, name="sum")(parts)

    summed, on, off = together((sum_up(parts), on, off))
    parts = column(summed)
    off, on = swap_off(off), swap_on(on)
    grad_state = call(
        finish_body, sds((LAT, LON, CH), BF), 3, bytes_accessed=1 << 20, name="finish", scalars=1
    )(core, off, on, gs)
    parts, grad_state = together((parts, grad_state))
    grad_disco, grad_obs = call(
        ending_body,
        (sds((K * CH, CH), F32), sds((CH, CH), F32)),
        1,
        bytes_accessed=1 << 18,
        name="ending",
    )(plane(sum_up(parts)).reshape(K * CH + CH, CH))
    return (
        output.reshape(LAT, LON, CH),
        grad_state,
        grad_disco.reshape(K, CH, CH),
        grad_obs,
    )


def solution(mesh):
    in_specs = (
        P(None, "tile", "chan"),
        P(("tile", "chan"), None),
        P(("tile", "chan"), None),
        P(("tile", "chan")),
        P(),
        P(),
        P(None, "chan"),
        P(None, None, "chan"),
        P(None, "tile", "chan"),
    )
    out_specs = (
        P(None, "tile", "chan"),
        P(None, "tile", "chan"),
        P(None, None, "chan"),
        P(None, "chan"),
    )
    return jax.shard_map(local, mesh=mesh, in_specs=in_specs, out_specs=out_specs, check_vma=False)
```

```python
import functools

import jax
import jax.numpy as jnp
from jax import lax
from jax.experimental import pallas as pl
from jax.experimental.pallas import tpu as pltpu
from jax.sharding import PartitionSpec as P

K = 3
J = 8
LAT = 40
LON = 32
CH = 128
CELLS = LAT * LON
ROWS = 512
TILES = 64
CAP = 16
PLANES = [[z * 8 + i for i in range(8)] for z in range(8)]
COLUMNS = [[z * 8 + i for z in range(8)] for i in range(8)]
SLOT = 18
PACK = TILES * SLOT
BF = jnp.bfloat16
F32 = jnp.float32
tanh_scale = 0.7978845608028654
cubic_weight = 0.044715
GRID_SCALE = float(CELLS * TILES) ** -0.5
OBS_SCALE = float(ROWS * TILES * 4) ** -0.5

VM = pl.BlockSpec(memory_space=pltpu.VMEM)
SM = pl.BlockSpec(memory_space=pltpu.SMEM)
HB = pl.BlockSpec(memory_space=pltpu.HBM)


def call(body, outs, n_in, scratch=(), flops=0, bytes_accessed=0, name=None, space=VM, aliases=None, scalars=0, vmem=16, hbm=0):
    return pl.pallas_call(
        body,
        out_shape=outs,
        in_specs=[SM] * scalars + [HB] * hbm + [space] * n_in,
        out_specs=jax.tree.map(lambda _: VM, outs),
        scratch_shapes=list(scratch),
        compiler_params=pltpu.CompilerParams(vmem_limit_bytes=vmem << 20),
        cost_estimate=pl.CostEstimate(
            flops=flops, bytes_accessed=bytes_accessed, transcendentals=0
        ),
        name=name,
        input_output_aliases=aliases or {},
    )


def sds(shape, dtype):
    return jax.ShapeDtypeStruct(shape, dtype)


def iota(shape, dim):
    return lax.broadcasted_iota(jnp.int32, shape, dim)


def one(mask):
    return jnp.where(mask, 1.0, 0.0).astype(BF)


def dot(a, b, ca=1, cb=0):
    return lax.dot_general(a, b, (((ca,), (cb,)), ((), ())), preferred_element_type=F32)


def pack_body(obs_hbm, tile_hbm, cell_hbm, out_ref, obs_ref, tile_ref, cell_ref, sems):
    copies = [
        pltpu.make_async_copy(src, dst, sems.at[n])
        for n, (src, dst) in enumerate(
            ((tile_hbm, tile_ref), (cell_hbm, cell_ref), (obs_hbm, obs_ref))
        )
    ]
    for copy in copies:
        copy.start()
    before = one(iota((ROWS, ROWS), 0) < iota((ROWS, ROWS), 1))
    for copy in copies:
        copy.wait()
    tile = tile_ref[...]
    cell = cell_ref[...]
    named = iota((TILES, ROWS), 0) == tile
    onehot = one(named)
    counts = dot(onehot, before)
    rank = jnp.sum(jnp.where(named, counts, 0.0), axis=0, keepdims=True).astype(jnp.int32)
    place = one(iota((PACK, ROWS), 0) == tile * SLOT + rank)
    high = (cell >> 5).astype(F32)
    low = (cell & 31).astype(F32)
    lane = iota((CH, ROWS), 0)
    marks = jnp.where(lane == rank, high, 0.0) + jnp.where(lane == rank + CAP, low, 0.0)
    marks = dot(onehot, marks.astype(BF), 1, 1)
    mark_place = one(iota((PACK, TILES), 0) == iota((PACK, TILES), 1) * SLOT + CAP)
    packed = dot(place, obs_ref[...]) + dot(mark_place, marks.astype(BF))
    out_ref[...] = packed.astype(BF)


def add_block(block_ref, store):
    block = block_ref[...]
    rows = block.shape[0]
    q = iota((CH, rows), 1)
    t18 = iota((CH, rows), 0) * SLOT
    marks = dot(one(q == t18 + CAP), block)
    marks = marks.T.astype(BF)
    spread = one((q >= t18) & (q < t18 + SLOT))
    wide = dot(marks[: 2 * CAP], spread)
    qf = iota((CAP, rows), 1).astype(F32)
    within = qf - SLOT * jnp.floor((qf + 0.5) * (1.0 / SLOT))
    mine = within == iota((CAP, rows), 0).astype(F32)
    high = jnp.sum(jnp.where(mine, wide[:CAP], 0.0), axis=0, keepdims=True)
    low = jnp.sum(jnp.where(mine, wide[CAP:], 0.0), axis=0, keepdims=True)
    high = jnp.where(within[:1] > CAP - 0.5, -1.0, high)
    lows = jnp.where(iota((LON, rows), 0).astype(F32) == low, 1.0, 0.0)
    for c in range(0, LAT, 8):
        hot = jnp.concatenate(
            [jnp.where(high == float(i), lows, 0.0).astype(BF) for i in range(c, c + 8)], axis=0
        )
        store(slice(c * LON, (c + 8) * LON), dot(hot, block))


def deposit_first(block_ref, acc_ref):
    def store(rows, part):
        acc_ref[rows] = part

    add_block(block_ref, store)


def side_columns(core_ref):
    on = (1 - core_ref[0]) * (LON - 2)
    off = core_ref[0] * (LON - 2)
    return (on, on + 1, off, off + 1)


def take_sides(core_ref, cells_ref, out_ref):
    for n, at in enumerate(side_columns(core_ref)):
        out_ref[n * LAT : (n + 1) * LAT] = cells_ref[pl.ds(at, LAT, stride=LON), :]


def sides_body(core_ref, state_ref, out_ref, wide):
    wide[...] = state_ref[...].astype(F32)
    take_sides(core_ref, wide, out_ref)


def deposit_pair(core_ref, block_ref, acc_in, acc_ref, send_ref, side_ref, side_send_ref):
    def store(rows, part):
        total = acc_in[rows] + part
        acc_ref[rows] = total
        send_ref[rows] = total.astype(BF)

    add_block(block_ref, store)
    take_sides(core_ref, acc_ref, side_ref)
    side_send_ref[...] = side_ref[...].astype(BF)


def edges_body(side_ref, other_ref, state_ref, we_ref, on_ref, off_ref):
    sums = (side_ref[...] + other_ref[...].astype(F32)).astype(BF)
    mixed = (state_ref[...] + dot(sums, we_ref[...])).astype(BF)
    both = jnp.concatenate([mixed, sums], axis=1)
    on_ref[...] = both[: 2 * LAT]
    off_ref[...] = both[2 * LAT :]


def filter_body(quad_ref, near_ref, m_ref, mt_ref, edge_ref, v_ref):
    quad = quad_ref[...]
    near = near_ref[...]
    near = jnp.concatenate([near] * K, axis=0)
    lane = iota((K * LAT, CH), 1)
    coupling = jnp.zeros((K * LAT, CH), F32)
    for j in range(J):
        coupling += jnp.where(near[:, j : j + 1] == lane, quad[:, j : j + 1], 0.0)
    ahead = iota((LAT, 4 * LAT), 1) - iota((LAT, 4 * LAT), 0)
    row = iota((LAT, 4 * LAT), 0)
    parts = []
    links = {0: ((0, 0), (1, 1)), 1: ((1, 0),), 2: ((2, 4),), 3: ((2, 3), (3, 4))}
    for k in range(K):
        for e in range(4):
            part = jnp.zeros((LAT, 4 * LAT), F32)
            for h, b in links[e]:
                for step in range(3):
                    ok = (ahead == LAT * h + step - 1) & (row + (step - 1) >= 0) & (row + (step - 1) < LAT)
                    o = step * 5 + b
                    part += jnp.where(ok, coupling[k * LAT : (k + 1) * LAT, o : o + 1], 0.0)
            parts.append(part)
    edge_ref[...] = jnp.concatenate(parts, axis=0).astype(BF)
    coupling = coupling.astype(BF)

    def column(at):
        edge = at - 96
        step = jnp.where(at < 96, at >> 5, edge >> 2)
        side = edge & 3
        col = jnp.where(at < 96, at & 31, jnp.where(side < 2, side - 2, side + 30))
        return step, jnp.where(at < 108, col, -99)

    step, _ = column(iota((CH, CH), 1))
    for b in range(5):
        v_ref[:, b * CH : (b + 1) * CH] = dot(coupling, one(iota((CH, CH), 0) == step * 5 + b))
    _, col = column(iota((LON, CH), 1))
    masks = [
        jnp.where(col == iota((LON, CH), 0) + (b - 2), 1.0, 0.0) for b in range(5)
    ]

    def one_row(i, _):
        parts = []
        for k in range(K):
            row = v_ref[pl.ds(k * LAT + i, 1), :]
            part = masks[0] * row[:, :CH]
            for b in range(1, 5):
                part += masks[b] * row[:, b * CH : (b + 1) * CH]
            parts.append(part)
        whole = jnp.concatenate(parts, axis=0)
        m_ref[i] = jnp.where(iota((K * LON, CH), 1) < 3 * LON, whole, 0.0).astype(BF)
        whole = jnp.concatenate([whole, jnp.zeros((CH - K * LON, CH), F32)], axis=0)
        mt_ref[i] = whole.T.astype(BF)
        return 0

    lax.fori_loop(0, LAT, one_row, 0, unroll=8)


def own_body(
    m_ref, acc_ref, other_ref, state_ref, we_ref, cot_ref,
    mixed_ref, basis_ref, bat_ref, acot_ref,
    xp, ba,
):
    top = LON + CELLS
    xp[:LON] = jnp.zeros((LON, 2 * CH), BF)
    we = we_ref[...]
    for c in range(0, CELLS, 256):
        rows = slice(c, c + 256)
        a = (acc_ref[rows] + other_ref[rows].astype(F32)).astype(BF)
        mixed = (state_ref[rows].astype(F32) + dot(a, we)).astype(BF)
        mixed_ref[rows] = mixed
        xp[LON + c : LON + c + 256, :CH] = mixed
        xp[LON + c : LON + c + 256, CH:] = a
    xp[top:] = jnp.zeros((3 * LON, 2 * CH), BF)

    def gather(i, _):
        at = pl.multiple_of(i * LON, LON)
        part = dot(m_ref[i], xp[pl.ds(at, CH)])
        for k in range(K):
            rows = slice(k * LON, (k + 1) * LON)
            basis_ref[pl.ds(k * CELLS + at, LON)] = part[rows, :CH]
            ba[pl.ds(at, LON), k * CH : (k + 1) * CH] = part[rows, CH:].astype(BF)
        return 0

    lax.fori_loop(0, LAT, gather, 0, unroll=40)
    for k in range(K):
        for c in range(0, CELLS, 256):
            bat_ref[:, k * CELLS + c : k * CELLS + c + 256] = ba[
                c : c + 256, k * CH : (k + 1) * CH
            ].T
    acot_ref[...] = dot(xp[LON:top, CH:], cot_ref[...], 0, 0)


def block_body(
    core_ref, on_ref, off_ref, basis_in, bat_ref, acot_ref, edge_ref, mixed_ref, cot_ref, wd_ref,
    basis_ref, out_ref, back_ref, g_ref,
    slope_f, slopes, some_ref,
):
    del basis_in
    even = core_ref[0] == 0
    on, off = on_ref[...], off_ref[...]
    halo = jnp.concatenate([jnp.where(even, off, on), jnp.where(even, on, off)], axis=0)
    from_halo = dot(edge_ref[...], halo)
    for k in range(K):
        for e, at in enumerate((0, 1, LON - 2, LON - 1)):
            rows = pl.ds(k * CELLS + at, LAT, stride=LON)
            n = (k * 4 + e) * LAT
            basis_ref[rows, :] = basis_ref[rows, :] + from_halo[n : n + LAT, :CH]
    wd = wd_ref[...]
    for c in range(0, CELLS, 256):
        rows = slice(c, c + 256)
        some = jnp.concatenate(
            [basis_ref[k * CELLS + c : k * CELLS + c + 256].astype(BF) for k in range(K)], axis=1
        )
        some_ref[rows] = some
        v = dot(some, wd)
        square = v * v
        half = 0.5 + 0.5 * jnp.tanh(v * (tanh_scale + (tanh_scale * cubic_weight) * square))
        out_ref[rows] = (mixed_ref[rows].astype(F32) + v * half).astype(BF)
        rate = half + (v * half) * (1.0 - half) * (
            2.0 * tanh_scale + (6.0 * tanh_scale * cubic_weight) * square
        )
        slope = cot_ref[rows].astype(F32) * rate
        slope_f[rows] = slope
        slope = slope.astype(BF)
        slopes[rows] = slope
        back = dot(slope, wd, 1, 1).astype(BF)
        for k in range(K):
            back_ref[k * CELLS + c : k * CELLS + c + 256] = back[:, k * CH : (k + 1) * CH]
    gd = dot(slopes[...], some_ref[...], 0, 0)
    g_ref[: K * CH] = (gd.T * GRID_SCALE).astype(BF)
    go = acot_ref[...] + dot(bat_ref[...], back_ref[...])
    sides = jnp.concatenate(
        [slope_f[pl.ds(at, LAT, stride=LON), :] for at in (0, 1, LON - 2, LON - 1)], axis=0
    ).astype(BF)
    back = dot(sides, wd, 1, 1).astype(BF)
    for k in range(K):
        some = from_halo[k * 4 * LAT : (k + 1) * 4 * LAT, CH:].astype(BF)
        go += dot(some, back[:, k * CH : (k + 1) * CH], 0, 0)
    g_ref[K * CH :] = (go * OBS_SCALE).astype(BF)


def spread_body(core_ref, mt_hbm, back_ref, cot_ref, gs_ref, on_ref, off_ref, tp, h3, mt_ref, sems):
    step = LAT // 5
    copies = [
        pltpu.make_async_copy(
            mt_hbm.at[c * step : (c + 1) * step], mt_ref.at[c * step : (c + 1) * step], sems.at[c]
        )
        for c in range(5)
    ]
    for copy in copies:
        copy.start()
    tp[...] = jnp.zeros((CELLS + 2 * LON, CH), F32)
    none = jnp.zeros((CH - K * LON, CH), BF)

    def scatter(i, _):
        at = pl.multiple_of(i * LON, LON)
        near = [back_ref[pl.ds(k * CELLS + at, LON)] for k in range(K)]
        part = dot(mt_ref[i], jnp.concatenate([*near, none], axis=0))
        tp[pl.ds(at, 3 * LON)] += part[: 3 * LON]
        h3[i] = part[3 * LON : 3 * LON + 16]
        return 0

    for c, copy in enumerate(copies):
        copy.wait()
        lax.fori_loop(c * step, (c + 1) * step, scatter, 0, unroll=8)
    gs_ref[...] = cot_ref[...].astype(F32) + tp[LON : LON + CELLS]
    pad = jnp.zeros((1, 16, CH), F32)
    side = jnp.concatenate([pad, h3[...], pad], axis=0)
    side = side[2:, 0:4] + side[1 : LAT + 1, 4:8] + side[:LAT, 8:12]
    even = core_ref[0] == 0
    left, right = side[:, :2], side[:, 2:]
    on_ref[...] = jnp.where(even, right, left)
    off_ref[...] = jnp.where(even, left, right)


def finish_body(core_ref, off_ref, on_ref, gs_ref, out_ref):
    even = core_ref[0] == 0
    on, off = on_ref[...], off_ref[...]
    left, right = jnp.where(even, off, on), jnp.where(even, on, off)
    full = jnp.concatenate([left, jnp.zeros((LAT, LON - 4, CH), F32), right], axis=1)
    out_ref[...] = (gs_ref[...].reshape(LAT, LON, CH) + full).astype(BF)


def sum_body(parts_ref, out_ref):
    total = jnp.sum(parts_ref[...].astype(F32), axis=0, keepdims=True).astype(BF)
    out_ref[...] = jnp.broadcast_to(total.astype(F32), out_ref.shape).astype(BF)


def ending_body(total_ref, disco_ref, obs_ref):
    disco_ref[...] = total_ref[: K * CH].astype(F32)
    obs_ref[...] = total_ref[K * CH :].astype(F32)


def local(
    state, obs_values, obs_tile, obs_cell, neighbours, quadrature, embed_weight, disco_weight,
    cotangent,
):
    exchange = functools.partial(
        lax.all_to_all, axis_name="tile", split_axis=0, concat_axis=0, tiled=True
    )
    plane = functools.partial(exchange, axis_index_groups=PLANES)
    column = functools.partial(exchange, axis_index_groups=COLUMNS)
    core = (lax.axis_index("tile") % 2).reshape(1)
    together = lax.optimization_barrier
    grid_rows = (CELLS, CH)
    cot = cotangent.reshape(grid_rows)
    packed = call(
        pack_body,
        sds((PACK, CH), BF),
        3,
        [
            pltpu.VMEM((ROWS, CH), BF),
            pltpu.VMEM((1, ROWS), jnp.int32),
            pltpu.VMEM((1, ROWS), jnp.int32),
            pltpu.SemaphoreType.DMA((3,)),
        ],
        flops=1 << 28,
        name="pack",
        space=HB,
        vmem=60,
    )(obs_values, obs_tile.reshape(1, ROWS), obs_cell.reshape(1, ROWS))
    packed, quadrature, neighbours, state = together((packed, quadrature, neighbours, state))
    state = state.reshape(grid_rows)
    mine = exchange(packed.reshape(TILES, SLOT // 2, 2, CH)).reshape(PACK, CH)
    sides = call(
        sides_body,
        sds((4 * LAT, CH), F32),
        1,
        [pltpu.VMEM(grid_rows, F32)],
        flops=1 << 28,
        name="sides",
        scalars=1,
    )(core, state)
    m, mt, edge = call(
        filter_body,
        (sds((LAT, K * LON, CH), BF), sds((LAT, CH, CH), BF), sds((K * 4 * LAT, 4 * LAT), BF)),
        2,
        [pltpu.VMEM((K * LAT, 5 * CH), F32)],
        flops=1 << 32,
        bytes_accessed=1 << 22,
        name="filters",
    )(quadrature.reshape(K * LAT, J), neighbours)
    mine, m, mt, edge, sides = together((mine, m, mt, edge, sides))

    def pair(x, turn):
        pairs = []
        for tile in range(TILES):
            flip = (1, 0, 3, 2) if (tile + turn) % 2 == 0 else (3, 2, 1, 0)
            pairs += [(tile * 4 + c, tile * 4 + flip[c]) for c in range(4)]
        return lax.ppermute(x, ("tile", "chan"), pairs)

    cost = dict(flops=2 * CELLS * PACK * CH, bytes_accessed=1 << 20)
    first = pair(mine, 0)
    acc = call(deposit_first, sds(grid_rows, F32), 1, name="deposit", **cost)(mine)
    acc, send, side, side_send = call(
        deposit_pair,
        (
            sds(grid_rows, F32),
            sds(grid_rows, BF),
            sds((4 * LAT, CH), F32),
            sds((4 * LAT, CH), BF),
        ),
        2,
        name="deposit_pair",
        scalars=1,
        **cost,
    )(core, first, acc)
    other_side = pair(side_send, 1)
    send, other_side = together((send, other_side))
    other = pair(send, 1)
    on, off = call(
        edges_body,
        (sds((2 * LAT, 2 * CH), BF), sds((2 * LAT, 2 * CH), BF)),
        4,
        flops=1 << 28,
        bytes_accessed=1 << 20,
        name="edges",
    )(side, other_side, sides, embed_weight)

    def swap_on(x):
        return lax.ppermute(x, "tile", [(t, t ^ 1) for t in range(TILES)])

    def swap_off(x):
        return lax.ppermute(
            x, "tile", [(t, (t + 1 if t % 2 else t - 1) % TILES) for t in range(TILES)]
        )

    on, off = swap_on(on), swap_off(off)
    mixed, basis, bat, acot = call(
        own_body,
        (
            sds(grid_rows, BF),
            sds((K * CELLS, CH), F32),
            sds((CH, K * CELLS), BF),
            sds((CH, CH), F32),
        ),
        6,
        [pltpu.VMEM((CELLS + 4 * LON, 2 * CH), BF), pltpu.VMEM((CELLS, K * CH), BF)],
        flops=1 << 31,
        bytes_accessed=1 << 22,
        name="own",
    )(m, acc, other, state, embed_weight, cot)
    _, output, back, grads = call(
        block_body,
        (
            sds((K * CELLS, CH), F32),
            sds(grid_rows, BF),
            sds((K * CELLS, CH), BF),
            sds((K * CH + CH, CH), BF),
        ),
        9,
        [
            pltpu.VMEM(grid_rows, F32),
            pltpu.VMEM(grid_rows, BF),
            pltpu.VMEM((CELLS, K * CH), BF),
        ],
        flops=1 << 30,
        bytes_accessed=1 << 22,
        name="block",
        aliases={3: 0},
        scalars=1,
    )(
        core, on, off, basis, bat, acot, edge, mixed, cot, disco_weight.reshape(K * CH, CH)
    )
    parts = plane(grads.reshape(8, 64, CH))
    gs, on, off = call(
        spread_body,
        (sds(grid_rows, F32), sds((LAT, 2, CH), F32), sds((LAT, 2, CH), F32)),
        2,
        [
            pltpu.VMEM((CELLS + 2 * LON, CH), F32),
            pltpu.VMEM((LAT, 16, CH), F32),
            pltpu.VMEM((LAT, CH, CH), BF),
            pltpu.SemaphoreType.DMA((5,)),
        ],
        flops=1 << 31,
        bytes_accessed=1 << 22,
        name="spread",
        scalars=1,
        hbm=1,
    )(core, mt, back, cot)
    parts, gs, on, off = together((parts, gs, on, off))
    def sum_up(parts):
        return call(sum_body, sds((8, 64, CH), BF), 1, bytes_accessed=1 << 18, name="sum")(parts)

    summed, on, off = together((sum_up(parts), on, off))
    parts = column(summed)
    off, on = swap_off(off), swap_on(on)
    grad_state = call(
        finish_body, sds((LAT, LON, CH), BF), 3, bytes_accessed=1 << 20, name="finish", scalars=1
    )(core, off, on, gs)
    parts, grad_state = together((parts, grad_state))
    grad_disco, grad_obs = call(
        ending_body,
        (sds((K * CH, CH), F32), sds((CH, CH), F32)),
        1,
        bytes_accessed=1 << 18,
        name="ending",
    )(plane(sum_up(parts)).reshape(K * CH + CH, CH))
    return (
        output.reshape(LAT, LON, CH),
        grad_state,
        grad_disco.reshape(K, CH, CH),
        grad_obs,
    )


def solution(mesh):
    in_specs = (
        P(None, "tile", "chan"),
        P(("tile", "chan"), None),
        P(("tile", "chan"), None),
        P(("tile", "chan")),
        P(),
        P(),
        P(None, "chan"),
        P(None, None, "chan"),
        P(None, "tile", "chan"),
    )
    out_specs = (
        P(None, "tile", "chan"),
        P(None, "tile", "chan"),
        P(None, None, "chan"),
        P(None, "chan"),
    )
    return jax.shard_map(local, mesh=mesh, in_specs=in_specs, out_specs=out_specs, check_vma=False)
```
